32 devices in a mesh: mem: 4 (over x, core), lon: 8 (over z, y).
Axes of the slice: x: 2, y: 2, z: 4, core: 2. Of those that a mesh axis runs over, the one named last changes fastest.
Arguments:
- controls: bfloat16 [2048, 32, 1024], P('lon', 'mem'), may hold values from -6 to 6
- perturbations: bfloat16 [2048, 32, 1024], P(None, 'mem', 'lon'), may hold values from -0.59765625 to 0.59765625
- lat_factor: bfloat16 [1024, 1024], P('mem'), may hold values from -0.09375 to 0.09375
- lon_factor: bfloat16 [2048, 2048], P('mem'), may hold values from -0.0625 to 0.0625
- obs_index: int32 [4, 8, 32768], P('mem', 'lon'), may hold values from 0 to 65535
- obs_weight: float32 [4, 8, 32768], P('mem', 'lon'), may hold values from 1 to 30
- obs_count: int32 [4, 8], P('mem', 'lon'), may hold values from 8193 to 32768, as said below
Outputs:
- hessian_product: float32 [2048, 32, 1024], P('lon', 'mem')
The draws below stay inside these ranges and needn't reach their ends.
Inputs may be any that keep to these rules, and one draw needn't show every extreme that they name: `obs_index`: several slots may name one grid point; grid points are numbered with latitude fastest within a tile of 512 by 128. `obs_count`: slots 0 to count - 1 of a tile are in use; some tile uses all 32768 slots.
All inputs are finite; a program needn't handle non-finite values.
Results may differ from the reference program's by a relative error of at most 0.008.
Values may be sent and summed in bfloat16 or wider, within the bound.
No kernel may reach another device: no remote copies, remote signals or barrier semaphores. Data moves between devices by JAX's collectives and lax.ppermute only.
A program may use at most 128 MiB of HBM per device.

```python
import math
import jax
import jax.numpy as jnp
from jax import lax

LON = 2048
LAT = 1024
K = 32
TILE_LON = 512
LAT_DEV = 128
TILE_CELLS = 65536
OBS_TILE = 32768
N_MEM = 4
N_LON = 8


def draw_obs_count(key, part):
    tile_rows = LON // TILE_LON
    tile_cols = LAT // LAT_DEV
    first_key, second_key = jax.random.split(jax.random.fold_in(key, 7))
    counted = jax.random.randint(first_key, (tile_rows * tile_cols,), OBS_TILE // 4 + 1, OBS_TILE + 1)
    chosen = jax.random.randint(second_key, (), 0, tile_rows * tile_cols)
    counted = jnp.where(jnp.arange(tile_rows * tile_cols) == chosen, OBS_TILE, counted)
    return counted.reshape(tile_rows, tile_cols).astype(jnp.int32)


def set_ends(array, rng, low, top_value):
    longest = array.shape.index(max(array.shape))
    spots = []
    for shift in (0, 1):
        where = [jax.random.randint(jax.random.fold_in(rng, axis), (), 0, length) for axis, length in enumerate(array.shape)]
        where[longest] = (where[longest] + shift) % array.shape[longest]
        spots.append(tuple(where))
    return array.at[spots[0]].set(low).at[spots[1]].set(top_value)


def spiked(array, stream_key, source, target, blocks, factor):
    def block_of(dim):
        return (jnp.arange(array.shape[dim]) // (array.shape[dim] // blocks)).reshape((-1,) + (1,) * (array.ndim - 1 - dim))

    near = jax.random.permutation(stream_key, blocks)[block_of(target)]
    other_side = (block_of(target) + blocks // 2) % blocks
    return jnp.where((block_of(source) == near) | (block_of(source) == other_side), factor * array, array)


def level_of(own_key, shape, pieces, smallest, high):
    gain, own = 1.0, jax.random.fold_in(own_key, 6)
    for position, shards_of in pieces:
        heights = jnp.exp(jax.random.uniform(jax.random.fold_in(own, position), (shards_of,), jnp.float32, smallest / len(pieces), high / len(pieces)))
        gain = gain * jnp.repeat(heights, shape[position] // shards_of).reshape([-1 if axis == position else 1 for axis in range(len(shape))])
    return gain


def noise(rng, shape, deviation, bound, cuts=(), held_as=jnp.bfloat16):
    values = deviation * jax.random.normal(rng, shape, jnp.float32)
    if cuts:
        values = values * level_of(rng, shape, cuts, -0.22, 0.18)
    return jnp.clip(values, -bound, bound).astype(held_as)


def bell_draw_with(own_key, extent, width, reach, cuts, heavy, kind=jnp.bfloat16):
    values = width * jax.random.normal(own_key, extent, jnp.float32)
    if cuts:
        values = values * level_of(own_key, extent, cuts, -0.22, 0.18)
    return jnp.clip(spiked(values, jax.random.fold_in(own_key, 3), *heavy), -reach, reach).astype(kind)


def setup_inputs(seed: int = 0) -> dict:
    key_list = jax.random.split(jax.random.key(seed), 8)
    return {
        "controls": noise(key_list[0], (LON, K, LAT), 1.0, 6.0, ((0, 8), (1, 4))),
        "perturbations": bell_draw_with(key_list[1], (LON, K, LAT), 0.1, 0.59765625, ((1, 4), (2, 8)), (1, 0, 4, 2.0)),
        "lat_factor": noise(key_list[2], (LAT, LAT), (4 * LAT) ** -0.5, 0.09375, ((0, 4),)),
        "lon_factor": noise(key_list[3], (LON, LON), (4 * LON) ** -0.5, 0.0625, ((0, 4),)),
        "obs_index": set_ends(jax.random.randint(key_list[4], (LON // TILE_LON, LAT // LAT_DEV, OBS_TILE), 0, TILE_CELLS), jax.random.fold_in(key_list[4], 1), 0, TILE_CELLS - 1).astype(jnp.int32),
        "obs_weight": jnp.clip(jnp.exp(math.log(30.0) - 3.4011974 * jax.random.uniform(key_list[5], (LON // TILE_LON, LAT // LAT_DEV, OBS_TILE), jnp.float32) ** level_of(key_list[5], (LON // TILE_LON, LAT // LAT_DEV, OBS_TILE), ((0, 4), (1, 8)), -0.2, 0.2)), 1.0, 30.0),
        "obs_count": draw_obs_count(jax.random.fold_in(key_list[7], 71), 0),
    }


def reference(controls, perturbations, lat_factor, lon_factor, obs_index, obs_weight, obs_count):
    members_first = jnp.moveaxis(controls, 1, 0)
    perturb_first = jnp.moveaxis(perturbations, 1, 0)

    def forward_step(running, inputs):
        control_row, perturb_row = inputs
        banded = (control_row.astype(jnp.float32) + lax.dot_general(control_row, lat_factor, (((1,), (1,)), ((), ())), preferred_element_type=jnp.float32)).astype(jnp.bfloat16)
        localized = banded.astype(jnp.float32) + jnp.dot(lon_factor, banded, preferred_element_type=jnp.float32)
        return running + perturb_row.astype(jnp.float32) * localized, None

    increment, _ = lax.scan(forward_step, jnp.zeros((LON, LAT), jnp.float32), (members_first, perturb_first))
    tile_lon = LON // N_MEM
    lat_band = LAT // N_LON
    tile_rows = jnp.arange(N_MEM, dtype=jnp.int32)[:, None, None]
    tile_cols = jnp.arange(N_LON, dtype=jnp.int32)[None, :, None]
    lon_at = tile_rows * tile_lon + obs_index // lat_band
    lat_at = tile_cols * lat_band + obs_index % lat_band
    flat_at = (lon_at * LAT + lat_at).reshape(-1)
    in_use = jnp.arange(OBS_TILE, dtype=jnp.int32)[None, None, :] < obs_count[:, :, None]
    picked = increment.reshape(-1)[flat_at].reshape(obs_weight.shape)
    values = jnp.where(in_use, obs_weight * picked, jnp.zeros_like(picked))
    gradient = jnp.zeros((LON * LAT,), jnp.float32).at[flat_at].add(values.reshape(-1)).reshape(LON, LAT).astype(jnp.bfloat16)

    def adjoint_member(inputs):
        control_row, perturb_row = inputs
        weighted = (perturb_row.astype(jnp.float32) * gradient.astype(jnp.float32)).astype(jnp.bfloat16)
        spread = (weighted.astype(jnp.float32) + lax.dot_general(lon_factor, weighted, (((0,), (0,)), ((), ())), preferred_element_type=jnp.float32)).astype(jnp.bfloat16)
        return control_row.astype(jnp.float32) + spread.astype(jnp.float32) + jnp.dot(spread, lat_factor, preferred_element_type=jnp.float32)

    result = lax.map(adjoint_member, (members_first, perturb_first))
    return jnp.moveaxis(result, 0, 1)
```

```python
import functools

import jax
import jax.numpy as jnp
from jax import lax
from jax.experimental import pallas as pl
from jax.experimental.pallas import tpu as pltpu
from jax.sharding import PartitionSpec as P

F32, BF16 = jnp.float32, jnp.bfloat16
ANY = pl.BlockSpec(memory_space=pl.ANY)


def weight_map_kernel(chunk, band, count_ref, index_ref, weight_ref, out_ref, acc_ref):
    step = pl.program_id(0)
    rows = acc_ref.shape[0]

    @pl.when(step == 0)
    def _():
        acc_ref[...] = jnp.zeros_like(acc_ref)

    slot = step * chunk + lax.broadcasted_iota(jnp.int32, (1, chunk), 1)
    index = index_ref[...]
    weight = jnp.where(slot < count_ref[0], weight_ref[...], 0.0)
    high = weight.astype(BF16).astype(F32)
    low = weight - high
    at_row = lax.broadcasted_iota(jnp.int32, (rows, chunk), 0) == index // band
    at_col = lax.broadcasted_iota(jnp.int32, (band, chunk), 0) == index % band
    picked = jnp.where(at_row, 1.0, 0.0).astype(BF16)
    spread = jnp.concatenate(
        [jnp.where(at_col, high, 0.0).astype(BF16), jnp.where(at_col, low, 0.0).astype(BF16)], axis=0
    )
    acc_ref[...] += lax.dot_general(
        picked, spread, (((1,), (1,)), ((), ())), preferred_element_type=F32
    )

    @pl.when(step == pl.num_programs(0) - 1)
    def _():
        out_ref[...] = acc_ref[:, :band] + acc_ref[:, band:]


def weight_map(obs_index, obs_weight, obs_count, rows, band):
    slots = obs_index.shape[-1]
    chunk = min(slots, 1024)
    return pl.pallas_call(
        functools.partial(weight_map_kernel, chunk, band),
        out_shape=jax.ShapeDtypeStruct((rows, band), F32),
        grid_spec=pltpu.PrefetchScalarGridSpec(
            num_scalar_prefetch=1,
            grid=(slots // chunk,),
            in_specs=[
                pl.BlockSpec((1, chunk), lambda i, c: (0, i)),
                pl.BlockSpec((1, chunk), lambda i, c: (0, i)),
            ],
            out_specs=pl.BlockSpec((rows, band), lambda i, c: (0, 0)),
            scratch_shapes=[pltpu.VMEM((rows, 2 * band), F32)],
        ),
        cost_estimate=pl.CostEstimate(
            flops=4 * rows * band * slots, bytes_accessed=8 * slots, transcendentals=0
        ),
        name="weight_map",
    )(obs_count.reshape(1), obs_index.reshape(1, slots), obs_weight.reshape(1, slots))


def low_lanes(shape):
    return lax.broadcasted_iota(jnp.int32, shape, 1) < shape[1] // 2


def swap(value):
    return pltpu.roll(value, value.shape[1] // 2, 1)


def pack(first, second, half):
    mask = low_lanes(first.shape)
    if half == 0:
        return jnp.where(mask, first, swap(second))
    return jnp.where(mask, swap(first), second)


def prepare_perturbations_kernel(members, x_ref, low_ref, high_ref, wide_ref):
    wide_ref[...] = x_ref[...].astype(F32)
    rows = low_ref.shape[0]
    lanes = x_ref.shape[1]
    for pair in range(members // 2):
        first = wide_ref[pl.ds(2 * pair, rows, stride=members), :]
        second = wide_ref[pl.ds(2 * pair + 1, rows, stride=members), :]
        where = slice(pair * lanes, (pair + 1) * lanes)
        low_ref[:, where] = pack(first, second, 0).astype(BF16)
        high_ref[:, where] = pack(first, second, 1).astype(BF16)


def prepare_perturbations(perturbations):
    lon_all, members, band = perturbations.shape
    rows = min(lon_all, 256)
    wide = members * band // 2
    return pl.pallas_call(
        functools.partial(prepare_perturbations_kernel, members),
        out_shape=[jax.ShapeDtypeStruct((lon_all, wide), BF16)] * 2,
        grid=(lon_all // rows,),
        in_specs=[pl.BlockSpec((rows * members, band), lambda i: (i, 0))],
        out_specs=[pl.BlockSpec((rows, wide), lambda i: (i, 0))] * 2,
        scratch_shapes=[pltpu.VMEM((rows * members, band), F32)],
        cost_estimate=pl.CostEstimate(
            flops=perturbations.size, bytes_accessed=4 * perturbations.size, transcendentals=0
        ),
        name="prepare_perturbations",
    )(perturbations.reshape(lon_all * members, band))


def prepare_controls_kernel(members, c_ref, out_ref, wide_ref):
    wide_ref[...] = c_ref[...].astype(F32)
    rows = out_ref.shape[1]
    for member in range(members):
        out_ref[member] = wide_ref[pl.ds(member, rows, stride=members), :].astype(BF16)


def prepare_controls(controls):
    lon_dev, members, lat_all = controls.shape
    lanes = 128
    return pl.pallas_call(
        functools.partial(prepare_controls_kernel, members),
        out_shape=jax.ShapeDtypeStruct((members, lon_dev, lat_all), BF16),
        grid=(lat_all // lanes,),
        in_specs=[pl.BlockSpec((lon_dev * members, lanes), lambda i: (0, i))],
        out_specs=pl.BlockSpec((members, lon_dev, lanes), lambda i: (0, 0, i)),
        scratch_shapes=[pltpu.VMEM((lon_dev * members, lanes), F32)],
        cost_estimate=pl.CostEstimate(
            flops=controls.size, bytes_accessed=4 * controls.size, transcendentals=0
        ),
        name="prepare_controls",
    )(controls.reshape(lon_dev * members, lat_all))


def banded_kernel(half, group, place, c_ref, *refs):
    lat_refs, out_refs = refs[:4], refs[4 : 4 + len(group)]
    all_ref, rows_ref = refs[4 + len(group) :]
    me, part = place[0], place[1]
    piece = lat_refs[0].shape[0]
    narrow = piece // 2

    @pl.when(pl.program_id(0) == 0)
    def _():
        for s in range(4):
            all_ref[pl.ds(s * piece, piece), :] = lat_refs[s][...]
        for j, s in enumerate(group):
            d = me ^ s
            start = ((d // 2) ^ part) * piece + (d % 2) * narrow
            rows_ref[pl.ds(j * narrow, narrow), :] = all_ref[
                pl.ds(pl.multiple_of(start, narrow), narrow), :
            ]

    product = [
        lax.dot_general(
            c_ref[i], rows_ref[...], (((1,), (1,)), ((), ())), preferred_element_type=F32
        )
        for i in range(2)
    ]
    lanes = 2 * narrow
    for j, s in enumerate(group):
        d = me ^ s
        where = pl.ds(pl.multiple_of(d * lanes, lanes), lanes)
        own = pack(c_ref[0, :, where].astype(F32), c_ref[1, :, where].astype(F32), half)
        block = slice((j // 2) * lanes, (j // 2 + 1) * lanes)
        term = pack(product[0][:, block], product[1][:, block], j % 2)
        out_refs[j][...] = (own + term).astype(BF16)


def banded(half, group, place, c_members, lat_parts):
    members, lon_dev, lat_all = c_members.shape
    piece = lat_parts[0].shape[0]
    lanes = piece
    count = len(group)
    return pl.pallas_call(
        functools.partial(banded_kernel, half, group),
        out_shape=[jax.ShapeDtypeStruct((lon_dev, members // 2 * lanes), BF16)] * count,
        grid_spec=pltpu.PrefetchScalarGridSpec(
            num_scalar_prefetch=1,
            grid=(members // 2,),
            in_specs=[pl.BlockSpec((2, lon_dev, lat_all), lambda i, p: (i, 0, 0))]
            + [pl.BlockSpec((piece, lat_all), lambda i, p: (0, 0))] * 4,
            out_specs=[pl.BlockSpec((lon_dev, lanes), lambda i, p: (0, i))] * count,
            scratch_shapes=[
                pltpu.VMEM((4 * piece, lat_all), BF16),
                pltpu.VMEM((count * piece // 2, lat_all), BF16),
            ],
        ),
        cost_estimate=pl.CostEstimate(
            flops=2 * lon_dev * members * lat_all * count * piece // 2,
            bytes_accessed=2 * c_members.size + 8 * piece * lat_all,
            transcendentals=0,
        ),
        name="banded",
    )(place, c_members, *lat_parts)


def increment_kernel(count, place, *refs):
    moved, lon_refs, x_hbm = refs[:count], refs[count : count + 4], refs[count + 4]
    send_ref, keep_ref = refs[count + 5 : count + 7]
    columns, lon_all_ref, x_ref, sum_ref, moved_sem, lon_sem, x_sem = refs[count + 7 :]
    me, part = place[0], place[1]
    lon_dev, wide = moved[0].shape
    depth = lon_refs[0].shape[0]
    lanes = sum_ref.shape[1]
    copies = []
    for s in range(count):
        rows = pl.ds(pl.multiple_of((me ^ s) * lon_dev, lon_dev), lon_dev)
        copies.append(pltpu.make_async_copy(moved[s], columns.at[rows, :], moved_sem.at[s]))
    lon_copies = []
    for s in range(4):
        rows = pl.ds(pl.multiple_of((part ^ s) * depth, depth), depth)
        lon_copies.append(
            pltpu.make_async_copy(lon_refs[s], lon_all_ref.at[rows, :], lon_sem.at[s])
        )
    x_copy = pltpu.make_async_copy(x_hbm, x_ref, x_sem)
    for copy in copies:
        copy.start()
    for copy in lon_copies:
        copy.start()
    x_copy.start()
    for copy in copies:
        copy.wait()
    block = min(depth, 256)
    for s in range(4):
        lon_copies[s].wait()
        if s == 0:
            x_copy.wait()

        def body(i, carry, s=s):
            start = pl.multiple_of((part ^ s) * depth + i * block, block)
            rows = pl.ds(start, block)
            total = jnp.zeros((block, lanes), F32)
            step = 256
            for c in range(0, wide, step):
                local = jnp.dot(
                    lon_all_ref[rows, :], columns[:, c : c + step], preferred_element_type=F32
                )
                local = local + columns[rows, c : c + step].astype(F32)
                local = local * x_ref[rows, c : c + step].astype(F32)
                for b in range(0, step, lanes):
                    total = total + local[:, b : b + lanes]
            sum_ref[rows, :] = total + swap(total)
            return carry

        lax.fori_loop(0, depth // block, body, 0)
    core = part % 2
    far = sum_ref.shape[0] // 2
    for ref, which in ((send_ref, 1 - core), (keep_ref, core)):
        low = sum_ref[pl.ds(pl.multiple_of(which * depth, depth), depth), :]
        high = sum_ref[pl.ds(pl.multiple_of(which * depth + far, depth), depth), :]
        ref[...] = jnp.where(low_lanes(low.shape), low, high)


def increment(place, moved, lon_parts, x_packed):
    count = len(moved)
    lon_all, wide = x_packed.shape
    depth = lon_parts[0].shape[0]
    lanes = 128
    return pl.pallas_call(
        functools.partial(increment_kernel, count),
        out_shape=[jax.ShapeDtypeStruct((depth, lanes), F32)] * 2,
        grid_spec=pltpu.PrefetchScalarGridSpec(
            num_scalar_prefetch=1,
            grid=(1,),
            in_specs=[ANY] * (count + 5),
            out_specs=[pl.BlockSpec((depth, lanes), lambda i, p: (0, 0))] * 2,
            scratch_shapes=[
                pltpu.VMEM((lon_all, wide), BF16),
                pltpu.VMEM((lon_all, lon_all), BF16),
                pltpu.VMEM((lon_all, wide), BF16),
                pltpu.VMEM((lon_all, lanes), F32),
                pltpu.SemaphoreType.DMA((count,)),
                pltpu.SemaphoreType.DMA((4,)),
                pltpu.SemaphoreType.DMA,
            ],
        ),
        cost_estimate=pl.CostEstimate(
            flops=2 * lon_all * lon_all * wide,
            bytes_accessed=2 * lon_all * lon_all + 4 * lon_all * wide,
            transcendentals=0,
        ),
        name="increment",
    )(place, *moved, *lon_parts, x_packed)


def spread_kernel(group, place, own_ref, other_ref, x_hbm, *refs):
    lon_refs, out_refs = refs[:4], refs[4 : 4 + len(group)]
    weighted, lon_all_ref, x_ref, lon_sem, x_sem = refs[4 + len(group) :]
    me, part = place[0], place[1]
    depth = lon_refs[0].shape[0]
    lon_dev, wide = out_refs[0].shape
    lanes = own_ref.shape[1]
    x_copy = pltpu.make_async_copy(x_hbm, x_ref, x_sem)
    x_copy.start()
    lon_copies = []
    for s in range(4):
        rows = pl.ds(pl.multiple_of((part ^ s) * depth, depth), depth)
        lon_copies.append(
            pltpu.make_async_copy(lon_refs[s], lon_all_ref.at[rows, :], lon_sem.at[s])
        )
    for copy in lon_copies:
        copy.start()
    x_copy.wait()
    core = part % 2
    for ref, which in ((own_ref, core), (other_ref, 1 - core)):
        packed = ref[...].astype(F32)
        swapped = swap(packed)
        mask = low_lanes(packed.shape)
        for high in range(2):
            both = jnp.where(mask, swapped, packed) if high else jnp.where(mask, packed, swapped)
            rows = pl.ds(pl.multiple_of((which + 2 * high) * depth, depth), depth)
            for b in range(0, wide, lanes):
                weighted[rows, b : b + lanes] = (
                    x_ref[rows, b : b + lanes].astype(F32) * both
                ).astype(BF16)
    for copy in lon_copies:
        copy.wait()
    for j, s in enumerate(group):
        start = pl.multiple_of((me ^ s) * lon_dev, lon_dev)
        block = lon_all_ref[:, pl.ds(start, lon_dev)]
        step = 256
        for c in range(0, wide, step):
            term = lax.dot_general(
                block,
                weighted[:, c : c + step],
                (((0,), (0,)), ((), ())),
                preferred_element_type=F32,
            )
            own = weighted[pl.ds(start, lon_dev), c : c + step].astype(F32)
            out_refs[j][:, c : c + step] = (own + term).astype(BF16)


def spread_back(group, place, own, other, x_packed, lon_parts, lon_dev):
    count = len(group)
    lon_all, wide = x_packed.shape
    depth, lanes = own.shape
    return pl.pallas_call(
        functools.partial(spread_kernel, group),
        out_shape=[jax.ShapeDtypeStruct((lon_dev, wide), BF16)] * count,
        grid_spec=pltpu.PrefetchScalarGridSpec(
            num_scalar_prefetch=1,
            grid=(1,),
            in_specs=[pl.BlockSpec((depth, lanes), lambda i, p: (0, 0))] * 2 + [ANY] * 5,
            out_specs=[pl.BlockSpec((lon_dev, wide), lambda i, p: (0, 0))] * count,
            scratch_shapes=[
                pltpu.VMEM((lon_all, wide), BF16),
                pltpu.VMEM((lon_all, lon_all), BF16),
                pltpu.VMEM((lon_all, wide), BF16),
                pltpu.SemaphoreType.DMA((4,)),
                pltpu.SemaphoreType.DMA,
            ],
        ),
        cost_estimate=pl.CostEstimate(
            flops=2 * lon_all * lon_dev * wide * count,
            bytes_accessed=2 * lon_all * lon_all + 4 * lon_all * wide,
            transcendentals=0,
        ),
        name="spread",
    )(place, own, other, x_packed, *lon_parts)


def finish_kernel(count, place, c_ref, *refs):
    first, second = refs[:count], refs[count : 2 * count]
    lat_low, lat_high = refs[2 * count : 2 * count + 4], refs[2 * count + 4 : 2 * count + 8]
    out_hbm, lat_ref, left_ref, stage_ref, out_sem = refs[2 * count + 8 :]
    me, part = place[0], place[1]
    members, rows, lat_all = c_ref.shape
    narrow = lat_low[0].shape[0] // 2
    lanes = 2 * narrow
    step, steps = pl.program_id(0), pl.num_programs(0)
    slot = step % 2
    blocks = lat_all // lanes

    def copy_out(at, slot, block):
        start = pl.multiple_of(at * members * rows, members * rows)
        return pltpu.make_async_copy(
            stage_ref.at[slot, block],
            out_hbm.at[pl.ds(start, members * rows), pl.ds(block * lanes, lanes)],
            out_sem.at[slot, block],
        )

    @pl.when(pl.program_id(0) == 0)
    def _():
        for s in range(4):
            for half, parts in enumerate((lat_low, lat_high)):
                for i in range(2):
                    start = (2 * (part ^ s) + i) * lanes + half * narrow
                    lat_ref[pl.ds(pl.multiple_of(start, narrow), narrow), :] = parts[s][
                        i * narrow : (i + 1) * narrow, :
                    ]

    for s in range(count):
        where = pl.ds(pl.multiple_of((me ^ s) * lanes, lanes), lanes)
        for pair in range(members // 2):
            block = slice(pair * lanes, (pair + 1) * lanes)
            low = first[s][:, block].astype(F32)
            high = second[s][:, block].astype(F32)
            for i in range(2):
                start = (2 * pair + i) * rows
                left_ref[start : start + rows, where] = pack(low, high, i).astype(BF16)

    @pl.when(step >= 2)
    def _():
        for block in range(blocks):
            copy_out(step - 2, slot, block).wait()

    wide = 256
    for c in range(0, lat_all, wide):
        product = jnp.dot(left_ref[...], lat_ref[:, c : c + wide], preferred_element_type=F32)
        for b in range(0, wide, lanes):
            block = (c + b) // lanes
            here = slice(c + b, c + b + lanes)
            for k in range(members):
                inside = slice(k * rows, (k + 1) * rows)
                stage_ref[slot, block, pl.ds(k, rows, stride=members), :] = (
                    product[inside, b : b + lanes]
                    + left_ref[inside, here].astype(F32)
                    + c_ref[k, :, here].astype(F32)
                )
            copy_out(step, slot, block).start()

    @pl.when(step == steps - 1)
    def _():
        for block in range(blocks):
            copy_out(step - 1, 1 - slot, block).wait()
        for block in range(blocks):
            copy_out(step, slot, block).wait()


def finish(place, c_members, first, second, lat_low, lat_high):
    members, lon_dev, lat_all = c_members.shape
    count = len(first)
    wide = first[0].shape[1]
    piece = lat_low[0].shape[0]
    rows = min(lon_dev, 64)
    return pl.pallas_call(
        functools.partial(finish_kernel, count),
        out_shape=jax.ShapeDtypeStruct((lon_dev * members, lat_all), F32),
        grid_spec=pltpu.PrefetchScalarGridSpec(
            num_scalar_prefetch=1,
            grid=(lon_dev // rows,),
            in_specs=[pl.BlockSpec((members, rows, lat_all), lambda i, p: (0, i, 0))]
            + [pl.BlockSpec((rows, wide), lambda i, p: (i, 0))] * (2 * count)
            + [pl.BlockSpec((piece, lat_all), lambda i, p: (0, 0))] * 8,
            out_specs=ANY,
            scratch_shapes=[
                pltpu.VMEM((lat_all, lat_all), BF16),
                pltpu.VMEM((members * rows, lat_all), BF16),
                pltpu.VMEM((2, lat_all // 128, members * rows, 128), F32),
                pltpu.SemaphoreType.DMA((2, lat_all // 128)),
            ],
        ),
        cost_estimate=pl.CostEstimate(
            flops=2 * members * lon_dev * lat_all * lat_all,
            bytes_accessed=8 * c_members.size,
            transcendentals=0,
        ),
        name="finish",
    )(place, c_members, *first, *second, *lat_low, *lat_high)


def exchange(value, axis, size, shift):
    return lax.ppermute(value, axis, [(i, i ^ shift) for i in range(size)])


def gathered(value):
    across = exchange(value, "mem", 4, 2)
    beside = exchange(value, "mem", 4, 1)
    return [value, beside, across, exchange(across, "mem", 4, 1)]


def local_fast(lon_parts_n, controls, perturbations, lat_factor, lon_factor, obs_index, obs_weight, obs_count):
    lon_dev, members, lat_all = controls.shape
    lon_all, _, band = perturbations.shape
    narrow = band // 2
    part, me = lax.axis_index("mem"), lax.axis_index("lon")
    place = jnp.stack([me, part]).astype(jnp.int32)
    shard = lat_factor.shape[0]
    split = lat_factor.reshape(shard // band, 2, narrow, lat_all)
    lat = [gathered(split[:, h].reshape(shard // 2, lat_all)) for h in range(2)]
    lon = gathered(lon_factor)
    c_members = prepare_controls(controls)
    x_packed = prepare_perturbations(perturbations)
    own_map = weight_map(obs_index, obs_weight, obs_count, lon_all // 4, band)
    other_map = exchange(own_map, "mem", 4, 2)
    first_side = part < 2
    low_map = jnp.where(first_side, own_map, other_map)
    high_map = jnp.where(first_side, other_map, own_map)

    far = tuple(range(lon_parts_n - 1, lon_parts_n // 2 - 1, -1))
    near = tuple(range(lon_parts_n // 2 - 1, -1, -1))

    def send_all(make):
        moved = [None] * lon_parts_n
        for group in (far, near):
            for s, block in zip(group, make(group)):
                moved[s] = exchange(block, "lon", lon_parts_n, s) if s else block
        return moved

    back = []
    forward = [
        send_all(lambda group: banded(h, group, place, c_members, lat[h])) for h in range(2)
    ]
    for h in range(2):
        send, keep = increment(place, forward[h], lon, x_packed[h])
        keep = keep + exchange(send, "mem", 4, 1)
        keep = keep + exchange(keep, "mem", 4, 2)
        cells = slice(h * narrow, (h + 1) * narrow)
        weights = jnp.concatenate([low_map[:, cells], high_map[:, cells]], axis=1)
        own = (keep * weights).astype(BF16)
        other = exchange(own, "mem", 4, 1)
        back.append(
            send_all(
                lambda group: spread_back(group, place, own, other, x_packed[h], lon, lon_dev)
            )
        )
    result = finish(place, c_members, back[0], back[1], lat[0], lat[1])
    return result.reshape(lon_dev, members, lat_all)


def local_plain(controls, perturbations, lat_factor, lon_factor, obs_index, obs_weight, obs_count):
    lon_dev, mem_dev, lat_all = controls.shape
    lat_full = lax.all_gather(lat_factor, "mem", axis=0, tiled=True)
    control_rows = controls.reshape(lon_dev * mem_dev, lat_all)
    band_rows = (
        control_rows.astype(F32)
        + lax.dot_general(
            control_rows, lat_full, (((1,), (1,)), ((), ())), preferred_element_type=F32
        )
    ).astype(BF16)
    moved = lax.all_to_all(
        band_rows.reshape(lon_dev, mem_dev, lat_all), "lon", split_axis=2, concat_axis=0, tiled=True
    )
    lon_all, _, lat_band = moved.shape
    columns = moved.reshape(lon_all, mem_dev * lat_band)
    lon_full = lax.all_gather(lon_factor, "mem", axis=0, tiled=True)
    localized = columns.astype(F32) + jnp.dot(lon_full, columns, preferred_element_type=F32)
    weighted_fwd = perturbations.reshape(lon_all, mem_dev * lat_band).astype(F32) * localized
    partial_sum = jnp.sum(weighted_fwd.reshape(lon_all, mem_dev, lat_band), axis=1)
    tile_sum = lax.psum_scatter(partial_sum, "mem", scatter_dimension=0, tiled=True)
    weights = weight_map(obs_index, obs_weight, obs_count, tile_sum.shape[0], lat_band)
    grad_tile = (tile_sum * weights).astype(BF16)
    gradient = lax.all_gather(grad_tile, "mem", axis=0, tiled=True)
    weighted = (
        (perturbations.astype(F32) * gradient.astype(F32)[:, None, :])
        .astype(BF16)
        .reshape(lon_all, mem_dev * lat_band)
    )
    back = lax.dot_general(
        lon_full, weighted, (((0,), (0,)), ((), ())), preferred_element_type=F32
    )
    spread = (weighted.astype(F32) + back).astype(BF16).reshape(lon_all, mem_dev, lat_band)
    returned = lax.all_to_all(spread, "lon", split_axis=0, concat_axis=2, tiled=True)
    back_rows = returned.reshape(lon_dev * mem_dev, lat_all)
    result = (
        control_rows.astype(F32)
        + back_rows.astype(F32)
        + jnp.dot(back_rows, lat_full, preferred_element_type=F32)
    )
    return result.reshape(lon_dev, mem_dev, lat_all)


def solution(mesh):
    in_specs = (
        P("lon", "mem", None),
        P(None, "mem", "lon"),
        P("mem", None),
        P("mem", None),
        P("mem", "lon", None),
        P("mem", "lon", None),
        P("mem", "lon"),
    )
    out_specs = P("lon", "mem", None)
    mem_parts, lon_parts_n = mesh.shape["mem"], mesh.shape["lon"]

    def local(controls, perturbations, lat_factor, *rest):
        lon_dev, members, lat_all = controls.shape
        lon_all, _, band = perturbations.shape
        fits = (
            mem_parts == 4
            and lon_parts_n == 8
            and band == 128
            and members == 8
            and lat_factor.shape[0] == 2 * band
            and lon_dev % 128 == 0
            and lon_all % 1024 == 0
        )
        plan = functools.partial(local_fast, lon_parts_n) if fits else local_plain
        return plan(controls, perturbations, lat_factor, *rest)

    return jax.shard_map(local, mesh=mesh, in_specs=in_specs, out_specs=out_specs, check_vma=False)
```

```python
import functools

import jax
import jax.numpy as jnp
from jax import lax
from jax.experimental import pallas as pl
from jax.experimental.pallas import tpu as pltpu
from jax.sharding import PartitionSpec as P


F32, BF16 = jnp.float32, jnp.bfloat16
ANY = pl.BlockSpec(memory_space=pl.ANY)


def weight_map_kernel(chunk, band, count_ref, index_ref, weight_ref, out_ref, acc_ref):
    step = pl.program_id(0)
    rows = acc_ref.shape[0]

    @pl.when(step == 0)
    def _():
        acc_ref[...] = jnp.zeros_like(acc_ref)

    slot = step * chunk + lax.broadcasted_iota(jnp.int32, (1, chunk), 1)
    index = index_ref[...]
    weight = jnp.where(slot < count_ref[0], weight_ref[...], 0.0)
    high = weight.astype(BF16).astype(F32)
    low = weight - high
    at_row = lax.broadcasted_iota(jnp.int32, (rows, chunk), 0) == index // band
    at_col = lax.broadcasted_iota(jnp.int32, (band, chunk), 0) == index % band
    picked = jnp.where(at_row, 1.0, 0.0).astype(BF16)
    spread = jnp.concatenate(
        [jnp.where(at_col, high, 0.0).astype(BF16), jnp.where(at_col, low, 0.0).astype(BF16)], axis=0
    )
    acc_ref[...] += lax.dot_general(
        picked, spread, (((1,), (1,)), ((), ())), preferred_element_type=F32
    )

    @pl.when(step == pl.num_programs(0) - 1)
    def _():
        out_ref[...] = acc_ref[:, :band] + acc_ref[:, band:]


def weight_map(obs_index, obs_weight, obs_count, rows, band):
    slots = obs_index.shape[-1]
    chunk = min(slots, 1024)
    return pl.pallas_call(
        functools.partial(weight_map_kernel, chunk, band),
        out_shape=jax.ShapeDtypeStruct((rows, band), F32),
        grid_spec=pltpu.PrefetchScalarGridSpec(
            num_scalar_prefetch=1,
            grid=(slots // chunk,),
            in_specs=[
                pl.BlockSpec((1, chunk), lambda i, c: (0, i)),
                pl.BlockSpec((1, chunk), lambda i, c: (0, i)),
            ],
            out_specs=pl.BlockSpec((rows, band), lambda i, c: (0, 0)),
            scratch_shapes=[pltpu.VMEM((rows, 2 * band), F32)],
        ),
        cost_estimate=pl.CostEstimate(
            flops=4 * rows * band * slots, bytes_accessed=8 * slots, transcendentals=0
        ),
        name="weight_map",
    )(obs_count.reshape(1), obs_index.reshape(1, slots), obs_weight.reshape(1, slots))


def low_lanes(shape):
    return lax.broadcasted_iota(jnp.int32, shape, 1) < shape[1] // 2


def swap(value):
    return pltpu.roll(value, value.shape[1] // 2, 1)


def pack(first, second, half):
    mask = low_lanes(first.shape)
    if half == 0:
        return jnp.where(mask, first, swap(second))
    return jnp.where(mask, swap(first), second)


def prepare_perturbations_kernel(members, x_ref, low_ref, high_ref, wide_ref):
    wide_ref[...] = x_ref[...].astype(F32)
    rows = low_ref.shape[0]
    lanes = x_ref.shape[1]
    for pair in range(members // 2):
        first = wide_ref[pl.ds(2 * pair, rows, stride=members), :]
        second = wide_ref[pl.ds(2 * pair + 1, rows, stride=members), :]
        where = slice(pair * lanes, (pair + 1) * lanes)
        low_ref[:, where] = pack(first, second, 0).astype(BF16)
        high_ref[:, where] = pack(first, second, 1).astype(BF16)


def prepare_perturbations(perturbations):
    lon_all, members, band = perturbations.shape
    rows = min(lon_all, 256)
    wide = members * band // 2
    return pl.pallas_call(
        functools.partial(prepare_perturbations_kernel, members),
        out_shape=[jax.ShapeDtypeStruct((lon_all, wide), BF16)] * 2,
        grid=(lon_all // rows,),
        in_specs=[pl.BlockSpec((rows * members, band), lambda i: (i, 0))],
        out_specs=[pl.BlockSpec((rows, wide), lambda i: (i, 0))] * 2,
        scratch_shapes=[pltpu.VMEM((rows * members, band), F32)],
        cost_estimate=pl.CostEstimate(
            flops=perturbations.size, bytes_accessed=4 * perturbations.size, transcendentals=0
        ),
        name="prepare_perturbations",
    )(perturbations.reshape(lon_all * members, band))


def prepare_controls_kernel(members, c_ref, out_ref, wide_ref):
    wide_ref[...] = c_ref[...].astype(F32)
    rows = out_ref.shape[1]
    for member in range(members):
        out_ref[member] = wide_ref[pl.ds(member, rows, stride=members), :].astype(BF16)


def prepare_controls(controls):
    lon_dev, members, lat_all = controls.shape
    lanes = 128
    return pl.pallas_call(
        functools.partial(prepare_controls_kernel, members),
        out_shape=jax.ShapeDtypeStruct((members, lon_dev, lat_all), BF16),
        grid=(lat_all // lanes,),
        in_specs=[pl.BlockSpec((lon_dev * members, lanes), lambda i: (0, i))],
        out_specs=pl.BlockSpec((members, lon_dev, lanes), lambda i: (0, 0, i)),
        scratch_shapes=[pltpu.VMEM((lon_dev * members, lanes), F32)],
        cost_estimate=pl.CostEstimate(
            flops=controls.size, bytes_accessed=4 * controls.size, transcendentals=0
        ),
        name="prepare_controls",
    )(controls.reshape(lon_dev * members, lat_all))


def latitude_rows(place, parts, all_ref, blocks, out_ref, columns=None):
    me, part = place[0], place[1]
    piece = next(iter(parts.values()))[0].shape[0]
    narrow = piece // 2
    halves = sorted({h for _, h in blocks})
    for at, h in enumerate(halves):
        for s in range(4):
            start = (at * 4 + s) * piece
            all_ref[start : start + piece, :] = parts[h][s][...]
    for j, (s, h) in enumerate(blocks):
        d = me ^ s
        start = (halves.index(h) * 4 + ((d // 2) ^ part)) * piece + (d % 2) * narrow
        rows = pl.ds(pl.multiple_of(start, narrow), narrow)
        here = slice(j * narrow, (j + 1) * narrow)
        if columns is None:
            out_ref[here, :] = all_ref[rows, :]
        else:
            for i, t in enumerate(columns):
                lanes = pl.ds(pl.multiple_of((me ^ t) * 2 * narrow, 2 * narrow), 2 * narrow)
                out_ref[here, i * 2 * narrow : (i + 1) * 2 * narrow] = all_ref[rows, lanes]


def banded_kernel(halves, group, place, c_ref, *refs):
    count = 4 * len(halves)
    parts = {h: refs[4 * i : 4 * i + 4] for i, h in enumerate(halves)}
    out_refs = refs[count : count + len(group)]
    all_ref, rows_ref, turned_ref = refs[count + len(group) :]
    me = place[0]
    blocks = [(s, h) for s in group for h in halves]
    lanes = parts[halves[0]][0].shape[0]

    @pl.when(pl.program_id(0) == 0)
    def _():
        latitude_rows(place, parts, all_ref, blocks, rows_ref)
        turned_ref[...] = rows_ref[...].T

    rows = c_ref.shape[1]
    left = c_ref[...].reshape(2 * rows, c_ref.shape[2])
    step = 256
    for c in range(0, turned_ref.shape[1], step):
        product = jnp.dot(left, turned_ref[:, c : c + step], preferred_element_type=F32)
        for b in range(0, step, lanes):
            for i in range(2):
                s, h = blocks[2 * (c + b) // lanes + i]
                where = pl.ds(pl.multiple_of((me ^ s) * lanes, lanes), lanes)
                own = pack(c_ref[0, :, where].astype(F32), c_ref[1, :, where].astype(F32), h)
                term = pack(product[:rows, b : b + lanes], product[rows:, b : b + lanes], i)
                out_refs[group.index(s)][halves.index(h)] = (own + term).astype(BF16)


def banded(halves, group, place, c_members, lat):
    members, lon_dev, lat_all = c_members.shape
    piece = lat[0][0].shape[0]
    lanes = piece
    count, cut = len(group), len(halves)
    blocks = count * cut
    parts = [part for h in halves for part in lat[h]]
    return pl.pallas_call(
        functools.partial(banded_kernel, halves, group),
        out_shape=[jax.ShapeDtypeStruct((cut, lon_dev, members // 2 * lanes), BF16)] * count,
        grid_spec=pltpu.PrefetchScalarGridSpec(
            num_scalar_prefetch=1,
            grid=(members // 2,),
            in_specs=[pl.BlockSpec((2, lon_dev, lat_all), lambda i, p: (i, 0, 0))]
            + [pl.BlockSpec((piece, lat_all), lambda i, p: (0, 0))] * len(parts),
            out_specs=[pl.BlockSpec((cut, lon_dev, lanes), lambda i, p: (0, 0, i))] * count,
            scratch_shapes=[
                pltpu.VMEM((len(parts) * piece, lat_all), BF16),
                pltpu.VMEM((blocks * piece // 2, lat_all), BF16),
                pltpu.VMEM((lat_all, blocks * piece // 2), BF16),
            ],
        ),
        cost_estimate=pl.CostEstimate(
            flops=lon_dev * members * lat_all * blocks * piece,
            bytes_accessed=2 * c_members.size + 2 * len(parts) * piece * lat_all,
            transcendentals=0,
        ),
        name="banded",
    )(place, c_members, *parts)


def increment_kernel(half, first, place, *refs):
    count = 8
    moved, lon_refs, x_hbm = refs[:count], refs[count : count + 2], refs[count + 2]
    rest = list(refs[count + 3 :])
    early_ref = None if first else rest.pop(0)
    outs = [rest.pop(0)] if first else [rest.pop(0), rest.pop(0)]
    columns, lon_ref, x_ref, sum_ref, moved_sem, lon_sem, x_sem = rest
    me, part = place[0], place[1]
    lon_dev, wide = moved[0].shape[1:]
    depth = lon_refs[0].shape[0]
    lanes = sum_ref.shape[2]
    shards = (0, 1) if first else (2, 3)
    copies = []
    for s in range(count):
        rows = pl.ds(pl.multiple_of((me ^ s) * lon_dev, lon_dev), lon_dev)
        from_ref = moved[s].at[half if moved[s].shape[0] > 1 else 0]
        copies.append(pltpu.make_async_copy(from_ref, columns.at[rows, :], moved_sem.at[s]))
    for i, s in enumerate(shards):
        rows = pl.ds(pl.multiple_of((part ^ s) * depth, depth), depth)
        copies.append(pltpu.make_async_copy(lon_refs[i], lon_ref.at[i], lon_sem.at[i]))
        copies.append(pltpu.make_async_copy(x_hbm.at[rows, :], x_ref.at[i], x_sem.at[i]))
    for copy in copies:
        copy.start()
    for copy in copies[: count + 2]:
        copy.wait()
    step = 256
    for i, s in enumerate(shards):
        if i:
            for copy in copies[count + 2 * i : count + 2 * i + 2]:
                copy.wait()
        rows = pl.ds(pl.multiple_of((part ^ s) * depth, depth), depth)
        total = None
        for c in range(0, wide, step):
            local = jnp.dot(lon_ref[i], columns[:, c : c + step], preferred_element_type=F32)
            local = local + columns[rows, c : c + step].astype(F32)
            local = local * x_ref[i, :, c : c + step].astype(F32)
            for b in range(0, step, lanes):
                term = local[:, b : b + lanes]
                total = term if total is None else total + term
        sum_ref[i] = total + swap(total)
    if first:
        outs[0][...] = sum_ref[...]
        return
    side = part // 2
    mask = low_lanes(outs[0].shape)
    flip = (jnp.where(mask, 0, 1) == side)
    for ref, i in ((outs[0], 1), (outs[1], 0)):
        ref[...] = jnp.where(flip, early_ref[i], sum_ref[i])


def increment(half, first, place, moved, lon_pair, x_packed, early=None):
    count = len(moved)
    lon_all, wide = x_packed.shape
    depth = lon_pair[0].shape[0]
    lanes = 128
    pair = jax.ShapeDtypeStruct((2, depth, lanes), F32)
    one = jax.ShapeDtypeStruct((depth, lanes), F32)
    pair_spec = pl.BlockSpec((2, depth, lanes), lambda i, p: (0, 0, 0))
    one_spec = pl.BlockSpec((depth, lanes), lambda i, p: (0, 0))
    return pl.pallas_call(
        functools.partial(increment_kernel, half, first),
        out_shape=pair if first else [one] * 2,
        grid_spec=pltpu.PrefetchScalarGridSpec(
            num_scalar_prefetch=1,
            grid=(1,),
            in_specs=[ANY] * (count + 3) + ([] if first else [pair_spec]),
            out_specs=pair_spec if first else [one_spec] * 2,
            scratch_shapes=[
                pltpu.VMEM((lon_all, wide), BF16),
                pltpu.VMEM((2, depth, lon_all), BF16),
                pltpu.VMEM((2, depth, wide), BF16),
                pltpu.VMEM((2, depth, lanes), F32),
                pltpu.SemaphoreType.DMA((count,)),
                pltpu.SemaphoreType.DMA((2,)),
                pltpu.SemaphoreType.DMA((2,)),
            ],
        ),
        cost_estimate=pl.CostEstimate(
            flops=4 * depth * lon_all * wide,
            bytes_accessed=4 * depth * lon_all + 4 * lon_all * wide,
            transcendentals=0,
        ),
        name="increment",
    )(place, *moved, *lon_pair, x_packed, *([] if first else [early]))


def turn_kernel(first_ref, second_ref, out_ref):
    depth = first_ref.shape[0]
    out_ref[:, :depth] = first_ref[...].T
    out_ref[:, depth:] = second_ref[...].T


def turned(first, second):
    depth, wide = first.shape
    step = 256
    return pl.pallas_call(
        turn_kernel,
        out_shape=jax.ShapeDtypeStruct((wide, 2 * depth), BF16),
        grid=(wide // step,),
        in_specs=[pl.BlockSpec((depth, step), lambda i: (0, i))] * 2,
        out_specs=pl.BlockSpec((step, 2 * depth), lambda i: (i, 0)),
        cost_estimate=pl.CostEstimate(
            flops=2 * depth * wide, bytes_accessed=8 * depth * wide, transcendentals=0
        ),
        name="turned",
    )(first, second)


def spread_kernel(halves, group, place, *refs):
    cut = len(halves)
    grads, x_hbm = refs[: 2 * cut], refs[2 * cut : 3 * cut]
    turned_refs, out_refs = refs[3 * cut : 3 * cut + 2], refs[3 * cut + 2 : 3 * cut + 2 + len(group)]
    weighted, left_ref, x_ref, left_sem, x_sem = refs[3 * cut + 2 + len(group) :]
    me, part = place[0], place[1]
    lon_dev, wide = out_refs[0].shape[1:]
    depth, lanes = grads[0].shape
    x_copies = [
        pltpu.make_async_copy(x_hbm[i], x_ref.at[i], x_sem.at[i]) for i in range(cut)
    ]
    for copy in x_copies:
        copy.start()
    copies = []
    for j, s in enumerate(group):
        rows = pl.ds(pl.multiple_of((me ^ s) * lon_dev, lon_dev), lon_dev)
        for t in range(4):
            to_lanes = pl.ds(pl.multiple_of((part ^ t) * depth, depth), depth)
            copies.append(
                pltpu.make_async_copy(
                    turned_refs[t // 2].at[rows, pl.ds((t % 2) * depth, depth)],
                    left_ref.at[pl.ds(j * lon_dev, lon_dev), to_lanes],
                    left_sem.at[j, t],
                )
            )
    for copy in copies:
        copy.start()
    core = part % 2
    for i in range(cut):
        x_copies[i].wait()
        for ref, which in ((grads[2 * i], core), (grads[2 * i + 1], 1 - core)):
            packed = ref[...].astype(F32)
            swapped = swap(packed)
            mask = low_lanes(packed.shape)
            for high in range(2):
                both = jnp.where(mask, swapped, packed) if high else jnp.where(mask, packed, swapped)
                rows = pl.ds(pl.multiple_of((which + 2 * high) * depth, depth), depth)
                for b in range(0, wide, lanes):
                    weighted[i, rows, b : b + lanes] = (
                        x_ref[i, rows, b : b + lanes].astype(F32) * both
                    ).astype(BF16)
    for copy in copies:
        copy.wait()
    step, tall = 256, 512
    for i in range(cut):
        for r in range(0, len(group) * lon_dev, tall):
            for c in range(0, wide, step):
                term = jnp.dot(
                    left_ref[r : r + tall, :],
                    weighted[i, :, c : c + step],
                    preferred_element_type=F32,
                )
                for b in range(0, tall, lon_dev):
                    j = (r + b) // lon_dev
                    rows = pl.ds(pl.multiple_of((me ^ group[j]) * lon_dev, lon_dev), lon_dev)
                    own = weighted[i, rows, c : c + step].astype(F32)
                    out_refs[j][i, :, c : c + step] = (own + term[b : b + lon_dev]).astype(BF16)


def spread_back(halves, group, place, grads, x_packed, turned_pair, lon_dev):
    count, cut = len(group), len(halves)
    lon_all, wide = x_packed[0].shape
    depth, lanes = grads[halves[0]][0].shape
    pieces = [piece for h in halves for piece in grads[h]]
    return pl.pallas_call(
        functools.partial(spread_kernel, halves, group),
        out_shape=[jax.ShapeDtypeStruct((cut, lon_dev, wide), BF16)] * count,
        grid_spec=pltpu.PrefetchScalarGridSpec(
            num_scalar_prefetch=1,
            grid=(1,),
            in_specs=[pl.BlockSpec((depth, lanes), lambda i, p: (0, 0))] * (2 * cut)
            + [ANY] * (cut + 2),
            out_specs=[pl.BlockSpec((cut, lon_dev, wide), lambda i, p: (0, 0, 0))] * count,
            scratch_shapes=[
                pltpu.VMEM((cut, lon_all, wide), BF16),
                pltpu.VMEM((count * lon_dev, lon_all), BF16),
                pltpu.VMEM((cut, lon_all, wide), BF16),
                pltpu.SemaphoreType.DMA((count, 4)),
                pltpu.SemaphoreType.DMA((cut,)),
            ],
        ),
        cost_estimate=pl.CostEstimate(
            flops=2 * lon_all * lon_dev * wide * count * cut,
            bytes_accessed=2 * lon_all * lon_dev * count + 4 * cut * lon_all * wide,
            transcendentals=0,
        ),
        name="spread",
    )(place, *pieces, *[x_packed[h] for h in halves], *turned_pair)


def contract_kernel(blocks, columns, members, place, base_ref, *refs):
    halves = sorted({h for _, h in blocks})
    sources = sorted({s for s, _ in blocks})
    count = len(sources)
    messages = dict(zip(sources, refs[:count]))
    refs = refs[count:]
    parts = {h: refs[4 * i : 4 * i + 4] for i, h in enumerate(halves)}
    refs = refs[4 * len(halves) :]
    me = place[0]
    rows = messages[sources[0]].shape[1]
    lanes = parts[halves[0]][0].shape[0]
    last = len(refs) == 5
    if last:
        out_hbm, all_ref, lat_ref, stage_ref, out_sem = refs
    else:
        out_ref, all_ref, lat_ref = refs
    step, steps = pl.program_id(0), pl.num_programs(0)
    slot = step % 2

    @pl.when(step == 0)
    def _():
        latitude_rows(place, parts, all_ref, blocks, lat_ref, columns)

    def copy_out(at, slot, i):
        start = pl.multiple_of(at * members * rows, members * rows)
        to_lanes = pl.ds(pl.multiple_of((me ^ columns[i]) * lanes, lanes), lanes)
        return pltpu.make_async_copy(
            stage_ref.at[slot, i],
            out_hbm.at[pl.ds(start, members * rows), to_lanes],
            out_sem.at[slot, i],
        )

    if last:

        @pl.when(step >= 2)
        def _():
            for i in range(len(columns)):
                copy_out(step - 2, slot, i).wait()

    def read(s, h, pair):
        ref = messages[s]
        at = h if ref.shape[0] > 1 else 0
        return ref[at, :, pair * lanes : (pair + 1) * lanes].astype(F32)

    left = []
    for member in range(members):
        line = []
        for j in range(0, len(blocks), 2):
            first, second = (read(*blocks[j + i], member // 2) for i in range(2))
            line.append(pack(first, second, member % 2).astype(BF16))
        left.append(jnp.concatenate(line, axis=1))
    left = jnp.concatenate(left, axis=0)
    wide = 256
    for c in range(0, len(columns) * lanes, wide):
        product = jnp.dot(left, lat_ref[:, c : c + wide], preferred_element_type=F32)
        for b in range(0, wide, lanes):
            i = (c + b) // lanes
            s = columns[i]
            mine = [h for t, h in blocks if t == s]
            for k in range(members):
                value = product[k * rows : (k + 1) * rows, b : b + lanes]
                if mine == [0, 1]:
                    value = value + pack(read(s, 0, k // 2), read(s, 1, k // 2), k % 2)
                elif mine:
                    packed = read(s, mine[0], k // 2)
                    if mine[0] != k % 2:
                        packed = swap(packed)
                    mask = low_lanes(packed.shape)
                    zero = jnp.zeros_like(packed)
                    value = value + (
                        jnp.where(mask, zero, packed) if mine[0] else jnp.where(mask, packed, zero)
                    )
                if last:
                    here = slice(i * lanes, (i + 1) * lanes)
                    stage_ref[slot, i, pl.ds(k, rows, stride=members), :] = (
                        value + base_ref[k, :, here]
                    )
                else:
                    where = pl.ds(pl.multiple_of((me ^ s) * lanes, lanes), lanes)
                    out_ref[k, :, i * lanes : (i + 1) * lanes] = value + base_ref[
                        k, :, where
                    ].astype(F32)
            if last:
                copy_out(step, slot, i).start()

    if last:

        @pl.when(step == steps - 1)
        def _():
            for i in range(len(columns)):
                copy_out(step - 1, 1 - slot, i).wait()
            for i in range(len(columns)):
                copy_out(step, slot, i).wait()


def contract(blocks, columns, place, base, messages, lat, last):
    members, lon_dev, lat_all = base.shape
    halves = sorted({h for _, h in blocks})
    sources = sorted({s for s, _ in blocks})
    piece = lat[0][0].shape[0]
    rows = min(lon_dev, 64)
    parts = [part for h in halves for part in lat[h]]
    moved = [messages[s] for s in sources]
    scratch = [
        pltpu.VMEM((len(parts) * piece, lat_all), BF16),
        pltpu.VMEM((len(blocks) * piece // 2, lat_all), BF16),
    ]
    if last:
        out_shape = jax.ShapeDtypeStruct((lon_dev * members, lat_all), F32)
        out_spec = ANY
        scratch += [
            pltpu.VMEM((2, lat_all // 128, members * rows, 128), F32),
            pltpu.SemaphoreType.DMA((2, lat_all // 128)),
        ]
    else:
        out_shape = jax.ShapeDtypeStruct(base.shape, F32)
        out_spec = pl.BlockSpec((members, rows, lat_all), lambda i, p: (0, i, 0))
    return pl.pallas_call(
        functools.partial(contract_kernel, blocks, columns, members),
        out_shape=out_shape,
        grid_spec=pltpu.PrefetchScalarGridSpec(
            num_scalar_prefetch=1,
            grid=(lon_dev // rows,),
            in_specs=[pl.BlockSpec((members, rows, lat_all), lambda i, p: (0, i, 0))]
            + [
                pl.BlockSpec((m.shape[0], rows, m.shape[2]), lambda i, p: (0, i, 0))
                for m in moved
            ]
            + [pl.BlockSpec((piece, lat_all), lambda i, p: (0, 0))] * len(parts),
            out_specs=out_spec,
            scratch_shapes=scratch,
        ),
        cost_estimate=pl.CostEstimate(
            flops=members * lon_dev * lat_all * len(blocks) * piece,
            bytes_accessed=8 * base.size,
            transcendentals=0,
        ),
        name="contract",
    )(place, base, *moved, *parts)


def exchange(value, axis, size, shift):
    return lax.ppermute(value, axis, [(i, i ^ shift) for i in range(size)])


FAR, NEAR = (7, 6, 5, 4), (3, 2, 1, 0)


def local_fast(controls, perturbations, lat_factor, lon_factor, obs_index, obs_weight, obs_count):
    return local_fast_body(
        controls, perturbations, lat_factor, lon_factor, obs_index, obs_weight, obs_count
    )


def local_fast_body(controls, perturbations, lat_factor, lon_factor, obs_index, obs_weight, obs_count):
    lon_dev, members, lat_all = controls.shape
    lon_all, _, band = perturbations.shape
    narrow = band // 2
    part, me = lax.axis_index("mem"), lax.axis_index("lon")
    place = jnp.stack([me, part]).astype(jnp.int32)
    shard = lat_factor.shape[0]
    split = lat_factor.reshape(shard // band, 2, narrow, lat_all)

    def gathered(value):
        across = exchange(value, "mem", 4, 2)
        beside = exchange(value, "mem", 4, 1)
        return [value, beside, across, exchange(across, "mem", 4, 1)]

    lat = [gathered(split[:, h].reshape(shard // 2, lat_all)) for h in range(2)]
    lon = gathered(lon_factor)
    c_members = prepare_controls(controls)
    x_packed = prepare_perturbations(perturbations)
    own_map = weight_map(obs_index, obs_weight, obs_count, lon_all // 4, band)
    other_map = exchange(own_map, "mem", 4, 2)
    first_side = part < 2
    low_map = jnp.where(first_side, own_map, other_map)
    high_map = jnp.where(first_side, other_map, own_map)

    def sent(group, blocks):
        return {s: exchange(block, "lon", 8, s) if s else block for s, block in zip(group, blocks)}

    far = [sent(FAR, banded((h,), FAR, place, c_members, lat)) for h in range(2)]
    near = sent(NEAR, banded((0, 1), NEAR, place, c_members, lat))
    turn = [turned(lon[2 * i], lon[2 * i + 1]) for i in range(2)]
    grads, back = [], []
    for h in range(2):
        moved = [(far[h] | near)[s] for s in range(8)]
        early = increment(h, True, place, moved, lon[:2], x_packed[h])
        send, keep = increment(h, False, place, moved, lon[2:], x_packed[h], early)
        keep = keep + exchange(send, "mem", 4, 1)
        keep = keep + exchange(keep, "mem", 4, 2)
        cells = slice(h * narrow, (h + 1) * narrow)
        weights = jnp.concatenate([low_map[:, cells], high_map[:, cells]], axis=1)
        own = (keep * weights).astype(BF16)
        grads.append((own, exchange(own, "mem", 4, 1)))
        blocks = spread_back((h,), FAR, place, {h: grads[h]}, x_packed, turn, lon_dev)
        back.append(sent(FAR, blocks))
    blocks = spread_back((0, 1), NEAR, place, dict(enumerate(grads)), x_packed, turn, lon_dev)
    back_near = sent(NEAR, blocks)
    columns = FAR + NEAR
    early_blocks = [(s, 0) for s in FAR] + [(s, h) for s in NEAR for h in range(2)]
    base = contract(early_blocks, columns, place, c_members, back[0] | back_near, lat, False)
    late_blocks = [(s, 1) for s in FAR]
    result = contract(late_blocks, columns, place, base, back[1], lat, True)
    return result.reshape(lon_dev, members, lat_all)


def local_plain(controls, perturbations, lat_factor, lon_factor, obs_index, obs_weight, obs_count):
    lon_dev, mem_dev, lat_all = controls.shape
    lat_full = lax.all_gather(lat_factor, "mem", axis=0, tiled=True)
    control_rows = controls.reshape(lon_dev * mem_dev, lat_all)
    band_rows = (
        control_rows.astype(F32)
        + lax.dot_general(
            control_rows, lat_full, (((1,), (1,)), ((), ())), preferred_element_type=F32
        )
    ).astype(BF16)
    moved = lax.all_to_all(
        band_rows.reshape(lon_dev, mem_dev, lat_all), "lon", split_axis=2, concat_axis=0, tiled=True
    )
    lon_all, _, lat_band = moved.shape
    columns = moved.reshape(lon_all, mem_dev * lat_band)
    lon_full = lax.all_gather(lon_factor, "mem", axis=0, tiled=True)
    localized = columns.astype(F32) + jnp.dot(lon_full, columns, preferred_element_type=F32)
    weighted_fwd = perturbations.reshape(lon_all, mem_dev * lat_band).astype(F32) * localized
    partial_sum = jnp.sum(weighted_fwd.reshape(lon_all, mem_dev, lat_band), axis=1)
    tile_sum = lax.psum_scatter(partial_sum, "mem", scatter_dimension=0, tiled=True)
    weights = weight_map(obs_index, obs_weight, obs_count, tile_sum.shape[0], lat_band)
    grad_tile = (tile_sum * weights).astype(BF16)
    gradient = lax.all_gather(grad_tile, "mem", axis=0, tiled=True)
    weighted = (
        (perturbations.astype(F32) * gradient.astype(F32)[:, None, :])
        .astype(BF16)
        .reshape(lon_all, mem_dev * lat_band)
    )
    back = lax.dot_general(
        lon_full, weighted, (((0,), (0,)), ((), ())), preferred_element_type=F32
    )
    spread = (weighted.astype(F32) + back).astype(BF16).reshape(lon_all, mem_dev, lat_band)
    returned = lax.all_to_all(spread, "lon", split_axis=0, concat_axis=2, tiled=True)
    back_rows = returned.reshape(lon_dev * mem_dev, lat_all)
    result = (
        control_rows.astype(F32)
        + back_rows.astype(F32)
        + jnp.dot(back_rows, lat_full, preferred_element_type=F32)
    )
    return result.reshape(lon_dev, mem_dev, lat_all)


def solution(mesh):
    in_specs = (
        P("lon", "mem", None),
        P(None, "mem", "lon"),
        P("mem", None),
        P("mem", None),
        P("mem", "lon", None),
        P("mem", "lon", None),
        P("mem", "lon"),
    )
    out_specs = P("lon", "mem", None)
    few = mesh.shape["mem"] == 4 and mesh.shape["lon"] == 8

    def local(controls, perturbations, lat_factor, *rest):
        lon_dev, members, _ = controls.shape
        lon_all, _, band = perturbations.shape
        fits = (
            few
            and band == 128
            and members == 8
            and lat_factor.shape[0] == 2 * band
            and lon_dev == 256
            and lon_all == 8 * lon_dev
        )
        plan = local_fast if fits else local_plain
        return plan(controls, perturbations, lat_factor, *rest)

    return jax.shard_map(local, mesh=mesh, in_specs=in_specs, out_specs=out_specs, check_vma=False)
```

```python
import functools

import jax
import jax.numpy as jnp
from jax import lax
from jax.experimental import pallas as pl
from jax.experimental.pallas import tpu as pltpu
from jax.sharding import PartitionSpec as P


F32, BF16 = jnp.float32, jnp.bfloat16
ANY = pl.BlockSpec(memory_space=pl.ANY)
VMEM = pl.BlockSpec(memory_space=pltpu.VMEM)
FAR, NEAR = (7, 6, 5, 4), (3, 2, 1, 0)


def weight_map_kernel(chunk, band, count_ref, index_ref, weight_ref, out_ref, acc_ref):
    step = pl.program_id(0)
    rows = acc_ref.shape[0]

    @pl.when(step == 0)
    def _():
        acc_ref[...] = jnp.zeros_like(acc_ref)

    slot = step * chunk + lax.broadcasted_iota(jnp.int32, (1, chunk), 1)
    index = index_ref[...]
    weight = jnp.where(slot < count_ref[0], weight_ref[...], 0.0)
    high = weight.astype(BF16).astype(F32)
    low = weight - high
    at_row = lax.broadcasted_iota(jnp.int32, (rows, chunk), 0) == index // band
    at_col = lax.broadcasted_iota(jnp.int32, (band, chunk), 0) == index % band
    picked = jnp.where(at_row, 1.0, 0.0).astype(BF16)
    spread = jnp.concatenate(
        [jnp.where(at_col, high, 0.0).astype(BF16), jnp.where(at_col, low, 0.0).astype(BF16)], axis=0
    )
    acc_ref[...] += lax.dot_general(
        picked, spread, (((1,), (1,)), ((), ())), preferred_element_type=F32
    )

    @pl.when(step == pl.num_programs(0) - 1)
    def _():
        out_ref[...] = acc_ref[:, :band] + acc_ref[:, band:]


def weight_map(obs_index, obs_weight, obs_count, rows, band):
    slots = obs_index.shape[-1]
    chunk = min(slots, 8192)
    return pl.pallas_call(
        functools.partial(weight_map_kernel, chunk, band),
        out_shape=jax.ShapeDtypeStruct((rows, band), F32),
        grid_spec=pltpu.PrefetchScalarGridSpec(
            num_scalar_prefetch=1,
            grid=(slots // chunk,),
            in_specs=[
                pl.BlockSpec((1, chunk), lambda i, c: (0, i)),
                pl.BlockSpec((1, chunk), lambda i, c: (0, i)),
            ],
            out_specs=pl.BlockSpec((rows, band), lambda i, c: (0, 0)),
            scratch_shapes=[pltpu.VMEM((rows, 2 * band), F32)],
        ),
        cost_estimate=pl.CostEstimate(
            flops=4 * rows * band * slots, bytes_accessed=8 * slots, transcendentals=0
        ),
        compiler_params=pltpu.CompilerParams(vmem_limit_bytes=40 << 20),
        name="weight_map",
    )(obs_count.reshape(1), obs_index.reshape(1, slots), obs_weight.reshape(1, slots))


def low_lanes(shape):
    return lax.broadcasted_iota(jnp.int32, shape, 1) < shape[1] // 2


def swap(value):
    return pltpu.roll(value, value.shape[1] // 2, 1)


def pack(first, second, half):
    mask = low_lanes(first.shape)
    if half == 0:
        return jnp.where(mask, first, swap(second))
    return jnp.where(mask, swap(first), second)


def prepare_perturbations_kernel(members, x_ref, low_ref, high_ref, wide_ref):
    wide_ref[...] = x_ref[...].astype(F32)
    rows = low_ref.shape[0]
    lanes = x_ref.shape[1]
    for pair in range(members // 2):
        first = wide_ref[pl.ds(2 * pair, rows, stride=members), :]
        second = wide_ref[pl.ds(2 * pair + 1, rows, stride=members), :]
        where = slice(pair * lanes, (pair + 1) * lanes)
        low_ref[:, where] = pack(first, second, 0).astype(BF16)
        high_ref[:, where] = pack(first, second, 1).astype(BF16)


def prepare_perturbations(perturbations):
    lon_all, members, band = perturbations.shape
    rows = min(lon_all, 256)
    wide = members * band // 2
    return pl.pallas_call(
        functools.partial(prepare_perturbations_kernel, members),
        out_shape=[jax.ShapeDtypeStruct((lon_all, wide), BF16)] * 2,
        grid=(lon_all // rows,),
        in_specs=[pl.BlockSpec((rows * members, band), lambda i: (i, 0))],
        out_specs=[pl.BlockSpec((rows, wide), lambda i: (i, 0))] * 2,
        scratch_shapes=[pltpu.VMEM((rows * members, band), F32)],
        cost_estimate=pl.CostEstimate(
            flops=perturbations.size, bytes_accessed=4 * perturbations.size, transcendentals=0
        ),
        compiler_params=pltpu.CompilerParams(vmem_limit_bytes=8 << 20),
        name="prepare_perturbations",
    )(perturbations.reshape(lon_all * members, band))


def prepare_controls_kernel(members, c_ref, out_ref, wide_ref):
    wide_ref[...] = c_ref[...].astype(F32)
    rows = out_ref.shape[1]
    for member in range(members):
        out_ref[member] = wide_ref[pl.ds(member, rows, stride=members), :].astype(BF16)


def prepare_controls(controls):
    lon_dev, members, lat_all = controls.shape
    lanes = 128
    return pl.pallas_call(
        functools.partial(prepare_controls_kernel, members),
        out_shape=jax.ShapeDtypeStruct((members, lon_dev, lat_all), BF16),
        grid=(lat_all // lanes,),
        in_specs=[pl.BlockSpec((lon_dev * members, lanes), lambda i: (0, i))],
        out_specs=pl.BlockSpec((members, lon_dev, lanes), lambda i: (0, 0, i)),
        scratch_shapes=[pltpu.VMEM((lon_dev * members, lanes), F32)],
        cost_estimate=pl.CostEstimate(
            flops=controls.size, bytes_accessed=4 * controls.size, transcendentals=0
        ),
        compiler_params=pltpu.CompilerParams(vmem_limit_bytes=8 << 20),
        name="prepare_controls",
    )(controls.reshape(lon_dev * members, lat_all))


def latitude_rows(place, parts, all_ref, blocks, out_ref, columns=None):
    me, part = place[0], place[1]
    piece = next(iter(parts.values()))[0].shape[0]
    narrow = piece // 2
    halves = sorted({h for _, h in blocks})
    for at, h in enumerate(halves):
        for s in range(4):
            start = (at * 4 + s) * piece
            all_ref[start : start + piece, :] = parts[h][s][...]
    for j, (s, h) in enumerate(blocks):
        d = me ^ s
        start = (halves.index(h) * 4 + ((d // 2) ^ part)) * piece + (d % 2) * narrow
        rows = pl.ds(pl.multiple_of(start, narrow), narrow)
        here = slice(j * narrow, (j + 1) * narrow)
        if columns is None:
            out_ref[here, :] = all_ref[rows, :]
        else:
            for i, t in enumerate(columns):
                lanes = pl.ds(pl.multiple_of((me ^ t) * 2 * narrow, 2 * narrow), 2 * narrow)
                out_ref[here, i * 2 * narrow : (i + 1) * 2 * narrow] = all_ref[rows, lanes]


def local_call(body, out_shape, scratch, flops, traffic, limit, out_spec=VMEM):
    outs = out_shape if isinstance(out_shape, list) else [out_shape]
    specs = [out_spec] * len(outs)

    def run(place, *args):
        return pl.pallas_call(
            body,
            out_shape=out_shape,
            in_specs=[pl.BlockSpec(memory_space=pltpu.SMEM)] + [VMEM] * len(args),
            out_specs=specs if isinstance(out_shape, list) else out_spec,
            scratch_shapes=scratch,
            cost_estimate=pl.CostEstimate(flops=flops, bytes_accessed=traffic, transcendentals=0),
            compiler_params=pltpu.CompilerParams(vmem_limit_bytes=limit << 20),
        )(place, *args)

    return run


def banded_kernel(halves, group, place, c_ref, *refs):
    count = 4 * len(halves)
    parts = {h: refs[4 * i : 4 * i + 4] for i, h in enumerate(halves)}
    out_refs = refs[count : count + len(group)]
    all_ref, rows_ref, turned_ref = refs[count + len(group) :]
    me = place[0]
    blocks = [(s, h) for s in group for h in halves]
    lanes = parts[halves[0]][0].shape[0]
    latitude_rows(place, parts, all_ref, blocks, rows_ref)
    turned_ref[...] = rows_ref[...].T
    members, rows, depth = c_ref.shape
    step = 256

    def body(pair, carry):
        left = c_ref[pl.ds(2 * pair, 2)].reshape(2 * rows, depth)
        to = pl.ds(pl.multiple_of(pair * lanes, lanes), lanes)
        for c in range(0, turned_ref.shape[1], step):
            product = jnp.dot(left, turned_ref[:, c : c + step], preferred_element_type=F32)
            for b in range(0, step, lanes):
                for i in range(2):
                    s, h = blocks[2 * (c + b) // lanes + i]
                    where = pl.ds(pl.multiple_of((me ^ s) * lanes, lanes), lanes)
                    own = pack(
                        c_ref[2 * pair, :, where].astype(F32),
                        c_ref[2 * pair + 1, :, where].astype(F32),
                        h,
                    )
                    term = pack(product[:rows, b : b + lanes], product[rows:, b : b + lanes], i)
                    out_refs[group.index(s)][halves.index(h), :, to] = (own + term).astype(BF16)
        return carry

    lax.fori_loop(0, members // 2, body, 0)


def banded(halves, group, place, c_members, lat):
    members, lon_dev, lat_all = c_members.shape
    piece = lat[0][0].shape[0]
    count, cut = len(group), len(halves)
    blocks = count * cut
    parts = [part for h in halves for part in lat[h]]
    return local_call(
        functools.partial(banded_kernel, halves, group),
        [jax.ShapeDtypeStruct((cut, lon_dev, members // 2 * piece), BF16)] * count,
        [
            pltpu.VMEM((len(parts) * piece, lat_all), BF16),
            pltpu.VMEM((blocks * piece // 2, lat_all), BF16),
            pltpu.VMEM((lat_all, blocks * piece // 2), BF16),
        ],
        lon_dev * members * lat_all * blocks * piece,
        2 * c_members.size + 2 * len(parts) * piece * lat_all,
        12,
    )(place, c_members, *parts)


def increment_kernel(half, place, *refs):
    moved, lon_refs, x_ref, outs = refs[:8], refs[8:12], refs[12], refs[13:15]
    columns, sum_ref = refs[15:]
    me, part = place[0], place[1]
    lon_dev, wide = moved[0].shape[1:]
    depth = lon_refs[0].shape[0]
    lanes = sum_ref.shape[2]
    for s in range(8):
        rows = pl.ds(pl.multiple_of((me ^ s) * lon_dev, lon_dev), lon_dev)
        columns[rows, :] = moved[s][half if moved[s].shape[0] > 1 else 0]
    step = 256
    for s in range(4):
        rows = pl.ds(pl.multiple_of((part ^ s) * depth, depth), depth)
        total = None
        for c in range(0, wide, step):
            local = jnp.dot(lon_refs[s][...], columns[:, c : c + step], preferred_element_type=F32)
            local = local + columns[rows, c : c + step].astype(F32)
            local = local * x_ref[rows, c : c + step].astype(F32)
            for b in range(0, step, lanes):
                term = local[:, b : b + lanes]
                total = term if total is None else total + term
        sum_ref[s] = total + swap(total)
    flip = jnp.where(low_lanes(outs[0].shape), 0, 1) == part // 2
    for ref, s in ((outs[0], 1), (outs[1], 0)):
        ref[...] = jnp.where(flip, sum_ref[s], sum_ref[s + 2])


def increment(half, place, moved, lon, x_packed):
    lon_all, wide = x_packed.shape
    depth = lon[0].shape[0]
    lanes = 128
    return local_call(
        functools.partial(increment_kernel, half),
        [jax.ShapeDtypeStruct((depth, lanes), F32)] * 2,
        [pltpu.VMEM((lon_all, wide), BF16), pltpu.VMEM((4, depth, lanes), F32)],
        2 * lon_all * lon_all * wide,
        2 * lon_all * lon_all + 4 * lon_all * wide,
        14,
    )(place, *moved, *lon, x_packed)


def weigh(place, grads, x_ref, weighted):
    part = place[1]
    depth, lanes = grads[0].shape
    wide = x_ref.shape[1]
    mark = jnp.where(low_lanes((depth, lanes)), 0, 1)
    for t in range(4):
        packed = grads[t % 2][...].astype(F32)
        both = jnp.where(mark == ((part // 2) ^ (t // 2)), packed, swap(packed))
        rows = pl.ds(pl.multiple_of((part ^ t) * depth, depth), depth)
        for b in range(0, wide, lanes):
            weighted[t * depth : (t + 1) * depth, b : b + lanes] = (
                x_ref[rows, b : b + lanes].astype(F32) * both
            ).astype(BF16)


def spread_kernel(group, first, place, *refs):
    if first:
        grads, x_ref, refs = refs[:2], refs[2], refs[3:]
        lon_refs, out_refs, weighted = refs[:4], refs[4:-1], refs[-1]
        weigh(place, grads, x_ref, weighted)
    else:
        weighted, lon_refs, out_refs = refs[0], refs[1:5], refs[5:]
    me, part = place[0], place[1]
    lon_dev = out_refs[0].shape[0]
    depth = lon_refs[0].shape[0]
    for j, s in enumerate(group):
        d = me ^ s
        columns = pl.ds(pl.multiple_of(d * lon_dev, lon_dev), lon_dev)
        start = ((d // 2) ^ part) * depth + (d % 2) * lon_dev
        total = weighted[pl.ds(pl.multiple_of(start, lon_dev), lon_dev), :].astype(F32)
        for t in range(4):
            total = total + lax.dot_general(
                lon_refs[t][:, columns],
                weighted[t * depth : (t + 1) * depth, :],
                (((0,), (0,)), ((), ())),
                preferred_element_type=F32,
            )
        out_refs[j][...] = total.astype(BF16)


def spread_back(group, first, place, inputs, lon, lon_dev):
    lon_all, wide = inputs[-1].shape
    count = len(group)
    block = jax.ShapeDtypeStruct((lon_dev, wide), BF16)
    outs = [block] * count + ([jax.ShapeDtypeStruct((lon_all, wide), BF16)] if first else [])
    return local_call(
        functools.partial(spread_kernel, group, first),
        outs,
        [],
        2 * lon_all * lon_dev * wide * count,
        2 * lon_all * lon_all + 4 * lon_all * wide,
        12,
    )(place, *inputs, *lon)


def contract_kernel(half, sources, members, last, place, base_ref, *refs):
    count = len(sources)
    messages, refs = refs[:count], refs[count:]
    parts, refs = {half: refs[:4]}, refs[4:]
    me = place[0]
    lanes = parts[half][0].shape[0]
    if last:
        out_hbm, all_ref, lat_ref, left_ref, stage_ref, out_sem = refs
    else:
        out_ref, all_ref, lat_ref, left_ref = refs
    latitude_rows(place, parts, all_ref, [(s, half) for s in sources], lat_ref, sources)
    rows = left_ref.shape[0] // members
    steps = base_ref.shape[1] // rows

    def copy_out(at, slot, i):
        start = pl.multiple_of(at * members * rows, members * rows)
        to_lanes = pl.ds(pl.multiple_of((me ^ sources[i]) * lanes, lanes), lanes)
        return pltpu.make_async_copy(
            stage_ref.at[slot, i],
            out_hbm.at[pl.ds(start, members * rows), to_lanes],
            out_sem.at[slot, i],
        )

    def body(step, carry):
        slot = step % 2
        here = pl.ds(pl.multiple_of(step * rows, rows), rows)
        if last:

            @pl.when(step >= 2)
            def _():
                for i in range(count):
                    copy_out(step - 2, slot, i).wait()

        def read(j, pair):
            return messages[j][here, pair * lanes : (pair + 1) * lanes].astype(F32)

        for member in range(members):
            for j in range(0, count, 2):
                both = pack(read(j, member // 2), read(j + 1, member // 2), member % 2)
                left_ref[
                    member * rows : (member + 1) * rows, j // 2 * lanes : (j // 2 + 1) * lanes
                ] = both.astype(BF16)
        wide = 256
        for c in range(0, count * lanes, wide):
            product = jnp.dot(left_ref[...], lat_ref[:, c : c + wide], preferred_element_type=F32)
            for b in range(0, wide, lanes):
                i = (c + b) // lanes
                where = pl.ds(pl.multiple_of((me ^ sources[i]) * lanes, lanes), lanes)
                for k in range(members):
                    value = product[k * rows : (k + 1) * rows, b : b + lanes]
                    packed = read(i, k // 2)
                    if half != k % 2:
                        packed = swap(packed)
                    mask = low_lanes(packed.shape)
                    zero = jnp.zeros_like(packed)
                    value = value + (
                        jnp.where(mask, zero, packed) if half else jnp.where(mask, packed, zero)
                    )
                    value = value + base_ref[k, here, where].astype(F32)
                    if last:
                        stage_ref[slot, i, pl.ds(k, rows, stride=members), :] = value
                    else:
                        out_ref[k, here, where] = value
                if last:
                    copy_out(step, slot, i).start()
        return carry

    lax.fori_loop(0, steps, body, 0)
    if last:
        for at in (steps - 2, steps - 1):
            for i in range(count):
                copy_out(at, at % 2, i).wait()


def contract(half, place, base, messages, lat, last):
    members, lon_dev, lat_all = base.shape
    sources = FAR + NEAR
    piece = lat[0][0].shape[0]
    rows = 64
    scratch = [
        pltpu.VMEM((4 * piece, lat_all), BF16),
        pltpu.VMEM((4 * piece, lat_all), BF16),
        pltpu.VMEM((members * rows, 4 * piece), BF16),
    ]
    if last:
        out_shape, out_spec = jax.ShapeDtypeStruct((lon_dev * members, lat_all), F32), ANY
        scratch += [
            pltpu.VMEM((2, len(sources), members * rows, piece), F32),
            pltpu.SemaphoreType.DMA((2, len(sources))),
        ]
    else:
        out_shape, out_spec = jax.ShapeDtypeStruct(base.shape, F32), VMEM
    return local_call(
        functools.partial(contract_kernel, half, sources, members, last),
        out_shape,
        scratch,
        members * lon_dev * lat_all * lat_all,
        8 * base.size,
        16,
        out_spec,
    )(place, base, *[messages[s] for s in sources], *lat[half])


def exchange(value, axis, size, shift):
    return lax.ppermute(value, axis, [(i, i ^ shift) for i in range(size)])


def local_fast(*args):
    return local_fast_body(*args)


def local_fast_body(controls, perturbations, lat_factor, lon_factor, obs_index, obs_weight, obs_count):
    lon_dev, members, lat_all = controls.shape
    lon_all, _, band = perturbations.shape
    narrow = band // 2
    part, me = lax.axis_index("mem"), lax.axis_index("lon")
    place = jnp.stack([me, part]).astype(jnp.int32)
    shard = lat_factor.shape[0]
    split = lat_factor.reshape(shard // band, 2, narrow, lat_all)

    def gathered(value):
        across = exchange(value, "mem", 4, 2)
        beside = exchange(value, "mem", 4, 1)
        return [value, beside, across, exchange(across, "mem", 4, 1)]

    lat = [gathered(split[:, h].reshape(shard // 2, lat_all)) for h in range(2)]
    lon = gathered(lon_factor)
    c_members = prepare_controls(controls)
    x_packed = prepare_perturbations(perturbations)
    own_map = weight_map(obs_index, obs_weight, obs_count, lon_all // 4, band)
    other_map = exchange(own_map, "mem", 4, 2)
    first_side = part < 2
    low_map = jnp.where(first_side, own_map, other_map)
    high_map = jnp.where(first_side, other_map, own_map)

    def sent(group, blocks):
        return {s: exchange(block, "lon", 8, s) if s else block for s, block in zip(group, blocks)}

    far = [sent(FAR, banded((h,), FAR, place, c_members, lat)) for h in range(2)]
    near = sent(NEAR, banded((0, 1), NEAR, place, c_members, lat))
    base = c_members
    for h in range(2):
        moved = [(far[h] | near)[s] for s in range(8)]
        send, keep = increment(h, place, moved, lon, x_packed[h])
        keep = keep + exchange(send, "mem", 4, 1)
        keep = keep + exchange(keep, "mem", 4, 2)
        cells = slice(h * narrow, (h + 1) * narrow)
        weights = jnp.concatenate([low_map[:, cells], high_map[:, cells]], axis=1)
        own = (keep * weights).astype(BF16)
        other = exchange(own, "mem", 4, 1)
        *blocks, weighted = spread_back(FAR, True, place, [own, other, x_packed[h]], lon, lon_dev)
        back = sent(FAR, blocks)
        blocks = spread_back(NEAR, False, place, [weighted], lon, lon_dev)
        back |= sent(NEAR, blocks)
        base = contract(h, place, base, back, lat, h == 1)
    return base.reshape(lon_dev, members, lat_all)


def local_plain(controls, perturbations, lat_factor, lon_factor, obs_index, obs_weight, obs_count):
    lon_dev, mem_dev, lat_all = controls.shape
    lat_full = lax.all_gather(lat_factor, "mem", axis=0, tiled=True)
    control_rows = controls.reshape(lon_dev * mem_dev, lat_all)
    band_rows = (
        control_rows.astype(F32)
        + lax.dot_general(
            control_rows, lat_full, (((1,), (1,)), ((), ())), preferred_element_type=F32
        )
    ).astype(BF16)
    moved = lax.all_to_all(
        band_rows.reshape(lon_dev, mem_dev, lat_all), "lon", split_axis=2, concat_axis=0, tiled=True
    )
    lon_all, _, lat_band = moved.shape
    columns = moved.reshape(lon_all, mem_dev * lat_band)
    lon_full = lax.all_gather(lon_factor, "mem", axis=0, tiled=True)
    localized = columns.astype(F32) + jnp.dot(lon_full, columns, preferred_element_type=F32)
    weighted_fwd = perturbations.reshape(lon_all, mem_dev * lat_band).astype(F32) * localized
    partial_sum = jnp.sum(weighted_fwd.reshape(lon_all, mem_dev, lat_band), axis=1)
    tile_sum = lax.psum_scatter(partial_sum, "mem", scatter_dimension=0, tiled=True)
    weights = weight_map(obs_index, obs_weight, obs_count, tile_sum.shape[0], lat_band)
    grad_tile = (tile_sum * weights).astype(BF16)
    gradient = lax.all_gather(grad_tile, "mem", axis=0, tiled=True)
    weighted = (
        (perturbations.astype(F32) * gradient.astype(F32)[:, None, :])
        .astype(BF16)
        .reshape(lon_all, mem_dev * lat_band)
    )
    back = lax.dot_general(
        lon_full, weighted, (((0,), (0,)), ((), ())), preferred_element_type=F32
    )
    spread = (weighted.astype(F32) + back).astype(BF16).reshape(lon_all, mem_dev, lat_band)
    returned = lax.all_to_all(spread, "lon", split_axis=0, concat_axis=2, tiled=True)
    back_rows = returned.reshape(lon_dev * mem_dev, lat_all)
    result = (
        control_rows.astype(F32)
        + back_rows.astype(F32)
        + jnp.dot(back_rows, lat_full, preferred_element_type=F32)
    )
    return result.reshape(lon_dev, mem_dev, lat_all)


def solution(mesh):
    in_specs = (
        P("lon", "mem", None),
        P(None, "mem", "lon"),
        P("mem", None),
        P("mem", None),
        P("mem", "lon", None),
        P("mem", "lon", None),
        P("mem", "lon"),
    )
    out_specs = P("lon", "mem", None)
    few = mesh.shape["mem"] == 4 and mesh.shape["lon"] == 8

    def local(controls, perturbations, lat_factor, *rest):
        lon_dev, members, _ = controls.shape
        lon_all, _, band = perturbations.shape
        fits = (
            few
            and band == 128
            and members == 8
            and lat_factor.shape[0] == 2 * band
            and lon_dev == 256
            and lon_all == 8 * lon_dev
        )
        plan = local_fast if fits else local_plain
        return plan(controls, perturbations, lat_factor, *rest)

    return jax.shard_map(local, mesh=mesh, in_specs=in_specs, out_specs=out_specs, check_vma=False)
```

```python
import functools

import jax
import jax.numpy as jnp
from jax import lax
from jax.experimental import pallas as pl
from jax.experimental.pallas import tpu as pltpu
from jax.sharding import PartitionSpec as P


F32, BF16 = jnp.float32, jnp.bfloat16
ANY = pl.BlockSpec(memory_space=pl.ANY)
VMEM = pl.BlockSpec(memory_space=pltpu.VMEM)
FAR, NEAR = (4, 5, 6, 7), (3, 2, 1, 0)
FIRST, SECOND = (4, 6), (5, 7)


def weight_map_kernel(chunk, band, count_ref, index_ref, weight_ref, out_ref, acc_ref):
    step = pl.program_id(0)
    rows = acc_ref.shape[0]

    @pl.when(step == 0)
    def _():
        acc_ref[...] = jnp.zeros_like(acc_ref)

    slot = step * chunk + lax.broadcasted_iota(jnp.int32, (1, chunk), 1)
    index = index_ref[...]
    weight = jnp.where(slot < count_ref[0], weight_ref[...], 0.0)
    high = weight.astype(BF16).astype(F32)
    low = weight - high
    at_row = lax.broadcasted_iota(jnp.int32, (rows, chunk), 0) == index // band
    at_col = lax.broadcasted_iota(jnp.int32, (band, chunk), 0) == index % band
    picked = jnp.where(at_row, 1.0, 0.0).astype(BF16)
    spread = jnp.concatenate(
        [jnp.where(at_col, high, 0.0).astype(BF16), jnp.where(at_col, low, 0.0).astype(BF16)], axis=0
    )
    acc_ref[...] += lax.dot_general(
        picked, spread, (((1,), (1,)), ((), ())), preferred_element_type=F32
    )

    @pl.when(step == pl.num_programs(0) - 1)
    def _():
        out_ref[...] = acc_ref[:, :band] + acc_ref[:, band:]


def weight_map(obs_index, obs_weight, obs_count, rows, band):
    slots = obs_index.shape[-1]
    chunk = min(slots, 8192)
    return pl.pallas_call(
        functools.partial(weight_map_kernel, chunk, band),
        out_shape=jax.ShapeDtypeStruct((rows, band), F32),
        grid_spec=pltpu.PrefetchScalarGridSpec(
            num_scalar_prefetch=1,
            grid=(slots // chunk,),
            in_specs=[
                pl.BlockSpec((1, chunk), lambda i, c: (0, i)),
                pl.BlockSpec((1, chunk), lambda i, c: (0, i)),
            ],
            out_specs=pl.BlockSpec((rows, band), lambda i, c: (0, 0)),
            scratch_shapes=[pltpu.VMEM((rows, 2 * band), F32)],
        ),
        cost_estimate=pl.CostEstimate(
            flops=4 * rows * band * slots, bytes_accessed=8 * slots, transcendentals=0
        ),
        compiler_params=pltpu.CompilerParams(vmem_limit_bytes=40 << 20),
        name="weight_map",
    )(obs_count.reshape(1), obs_index.reshape(1, slots), obs_weight.reshape(1, slots))


def low_lanes(shape):
    return lax.broadcasted_iota(jnp.int32, shape, 1) < shape[1] // 2


def swap(value):
    return pltpu.roll(value, value.shape[1] // 2, 1)


def pack(first, second, half):
    mask = low_lanes(first.shape)
    if half == 0:
        return jnp.where(mask, first, swap(second))
    return jnp.where(mask, swap(first), second)


def prepare_perturbations_kernel(members, x_ref, low_ref, high_ref, wide_ref):
    wide_ref[...] = x_ref[...].astype(F32)
    rows = low_ref.shape[0]
    lanes = x_ref.shape[1]
    for pair in range(members // 2):
        first = wide_ref[pl.ds(2 * pair, rows, stride=members), :]
        second = wide_ref[pl.ds(2 * pair + 1, rows, stride=members), :]
        where = slice(pair * lanes, (pair + 1) * lanes)
        low_ref[:, where] = pack(first, second, 0).astype(BF16)
        high_ref[:, where] = pack(first, second, 1).astype(BF16)


def prepare_perturbations(perturbations):
    lon_all, members, band = perturbations.shape
    rows = min(lon_all, 256)
    wide = members * band // 2
    return pl.pallas_call(
        functools.partial(prepare_perturbations_kernel, members),
        out_shape=[jax.ShapeDtypeStruct((lon_all, wide), BF16)] * 2,
        grid=(lon_all // rows,),
        in_specs=[pl.BlockSpec((rows * members, band), lambda i: (i, 0))],
        out_specs=[pl.BlockSpec((rows, wide), lambda i: (i, 0))] * 2,
        scratch_shapes=[pltpu.VMEM((rows * members, band), F32)],
        cost_estimate=pl.CostEstimate(
            flops=perturbations.size, bytes_accessed=4 * perturbations.size, transcendentals=0
        ),
        compiler_params=pltpu.CompilerParams(vmem_limit_bytes=8 << 20),
        name="prepare_perturbations",
    )(perturbations.reshape(lon_all * members, band))


def prepare_controls_kernel(c_hbm, out_ref, c_ref, wide_ref, sems):
    members, rows, _ = out_ref.shape
    blocks, _, lanes = c_ref.shape

    def fetch(i):
        here = pl.ds(i * lanes, lanes)
        return pltpu.make_async_copy(c_hbm.at[:, here], c_ref.at[i], sems.at[i])

    for i in range(blocks):
        fetch(i).start()
    for i in range(blocks):
        fetch(i).wait()
        wide_ref[i % 2] = c_ref[i].astype(F32)
        for member in range(members):
            out_ref[member, :, i * lanes : (i + 1) * lanes] = wide_ref[
                i % 2, pl.ds(member, rows, stride=members), :
            ].astype(BF16)


def prepare_controls(controls):
    lon_dev, members, lat_all = controls.shape
    lanes = 128
    blocks = lat_all // lanes
    return pl.pallas_call(
        prepare_controls_kernel,
        out_shape=jax.ShapeDtypeStruct((members, lon_dev, lat_all), BF16),
        in_specs=[pl.BlockSpec(memory_space=pltpu.HBM)],
        out_specs=VMEM,
        scratch_shapes=[
            pltpu.VMEM((blocks, lon_dev * members, lanes), BF16),
            pltpu.VMEM((2, lon_dev * members, lanes), F32),
            pltpu.SemaphoreType.DMA((blocks,)),
        ],
        cost_estimate=pl.CostEstimate(
            flops=controls.size, bytes_accessed=4 * controls.size, transcendentals=0
        ),
        compiler_params=pltpu.CompilerParams(vmem_limit_bytes=12 << 20),
    )(controls.reshape(lon_dev * members, lat_all))


def latitude_rows(place, parts, all_ref, blocks, out_ref, columns=None):
    me, part = place[0], place[1]
    offsets, filled = {}, 0
    for h, refs in parts.items():
        offsets[h] = filled
        for ref in refs:
            all_ref[filled : filled + ref.shape[0], :] = ref[...]
            filled += ref.shape[0]
    narrow = out_ref.shape[0] // len(blocks)
    for j, (s, h) in enumerate(blocks):
        shard, other = ((me ^ s) // 2) ^ part, s % 2
        if len(parts[h]) == 8:
            start = offsets[h] + (other * 4 + shard) * narrow
        elif parts[h][0].shape[0] == narrow:
            start = offsets[h] + shard * narrow
        else:
            start = offsets[h] + (shard * 2 + other) * narrow
        rows = pl.ds(pl.multiple_of(start, narrow), narrow)
        here = slice(j * narrow, (j + 1) * narrow)
        if columns is None:
            out_ref[here, :] = all_ref[rows, :]
        else:
            for i, t in enumerate(columns):
                lanes = pl.ds(pl.multiple_of((me ^ t) * 2 * narrow, 2 * narrow), 2 * narrow)
                out_ref[here, i * 2 * narrow : (i + 1) * 2 * narrow] = all_ref[rows, lanes]


def local_call(body, out_shape, scratch, flops, traffic, limit, out_spec=VMEM):
    outs = out_shape if isinstance(out_shape, list) else [out_shape]
    specs = [out_spec] * len(outs)

    def run(place, *args):
        return pl.pallas_call(
            body,
            out_shape=out_shape,
            in_specs=[pl.BlockSpec(memory_space=pltpu.SMEM)] + [VMEM] * len(args),
            out_specs=specs if isinstance(out_shape, list) else out_spec,
            scratch_shapes=scratch,
            cost_estimate=pl.CostEstimate(flops=flops, bytes_accessed=traffic, transcendentals=0),
            compiler_params=pltpu.CompilerParams(vmem_limit_bytes=limit << 20),
        )(place, *args)

    return run


def banded_kernel(halves, counts, group, members, place, c_ref, *refs):
    parts, at = {}, 0
    for h, count in zip(halves, counts):
        parts[h] = refs[at : at + count]
        at += count
    out_refs = refs[at : at + len(group)]
    all_ref, rows_ref, turned_ref, wide_ref = refs[at + len(group) :]
    me = place[0]
    blocks = [(s, h) for s in group for h in halves]
    tall, lanes = wide_ref.shape[1:]
    rows = tall // members
    latitude_rows(place, parts, all_ref, blocks, rows_ref)
    turned_ref[...] = rows_ref[...].T
    step = min(256, turned_ref.shape[1])

    def body(i, carry):
        here = pl.ds(pl.multiple_of(i * tall, tall), tall)
        to_rows = pl.ds(pl.multiple_of(i * rows, rows), rows)
        for c in range(0, turned_ref.shape[1], step):
            product = jnp.dot(
                c_ref[here, :], turned_ref[:, c : c + step], preferred_element_type=F32
            )
            for b in range(0, step, lanes):
                own = []
                for j in range(2):
                    s, h = blocks[2 * (c + b) // lanes + j]
                    where = pl.ds(pl.multiple_of((me ^ s) * lanes, lanes), lanes)
                    value = c_ref[here, where].astype(F32)
                    own.append(value if h == j else swap(value))
                wide = wide_ref.at[((c + b) // lanes) % wide_ref.shape[0]]
                wide[...] = product[:, b : b + lanes] + jnp.where(
                    low_lanes(own[0].shape), own[0], own[1]
                )
                for pair in range(members // 2):
                    first = wide[pl.ds(2 * pair, rows, stride=members), :]
                    second = wide[pl.ds(2 * pair + 1, rows, stride=members), :]
                    for j in range(2):
                        s, h = blocks[2 * (c + b) // lanes + j]
                        out_refs[group.index(s)][
                            halves.index(h), to_rows, pair * lanes : (pair + 1) * lanes
                        ] = pack(first, second, j).astype(BF16)
        return carry

    lax.fori_loop(0, c_ref.shape[0] // tall, body, 0)


def banded(halves, group, place, controls, parts):
    lon_dev, members, lat_all = controls.shape
    lanes = 128
    count, cut = len(group), len(halves)
    blocks = count * cut
    counts = [len(parts[h]) for h in halves]
    flat = [part for h in halves for part in parts[h]]
    staged = sum(part.shape[0] for part in flat)
    return local_call(
        functools.partial(banded_kernel, halves, counts, group, members),
        [jax.ShapeDtypeStruct((cut, lon_dev, members // 2 * lanes), BF16)] * count,
        [
            pltpu.VMEM((staged, lat_all), BF16),
            pltpu.VMEM((blocks * lanes // 2, lat_all), BF16),
            pltpu.VMEM((lat_all, blocks * lanes // 2), BF16),
            pltpu.VMEM((2, 64 * members, lanes), F32),
        ],
        lon_dev * members * lat_all * blocks * lanes,
        2 * controls.size + 2 * staged * lat_all,
        14,
    )(place, controls.reshape(lon_dev * members, lat_all), *flat)


def increment_kernel(half, place, *refs):
    moved, lon_refs, x_ref, outs = refs[:8], refs[8:12], refs[12], refs[13:15]
    columns, sum_ref = refs[15:]
    me, part = place[0], place[1]
    lon_dev, wide = moved[0].shape[1:]
    depth = lon_refs[0].shape[0]
    lanes = sum_ref.shape[2]
    for s in range(8):
        rows = pl.ds(pl.multiple_of((me ^ s) * lon_dev, lon_dev), lon_dev)
        columns[rows, :] = moved[s][half if moved[s].shape[0] > 1 else 0]
    step = 256
    for s in range(4):
        rows = pl.ds(pl.multiple_of((part ^ s) * depth, depth), depth)
        total = None
        for c in range(0, wide, step):
            local = jnp.dot(lon_refs[s][...], columns[:, c : c + step], preferred_element_type=F32)
            local = local + columns[rows, c : c + step].astype(F32)
            local = local * x_ref[rows, c : c + step].astype(F32)
            for b in range(0, step, lanes):
                term = local[:, b : b + lanes]
                total = term if total is None else total + term
        sum_ref[s] = total + swap(total)
    flip = jnp.where(low_lanes(outs[0].shape), 0, 1) == part // 2
    for ref, s in ((outs[0], 1), (outs[1], 0)):
        ref[...] = jnp.where(flip, sum_ref[s], sum_ref[s + 2])


def increment(half, place, moved, lon, x_packed):
    lon_all, wide = x_packed.shape
    depth = lon[0].shape[0]
    lanes = 128
    return local_call(
        functools.partial(increment_kernel, half),
        [jax.ShapeDtypeStruct((depth, lanes), F32)] * 2,
        [pltpu.VMEM((lon_all, wide), BF16), pltpu.VMEM((4, depth, lanes), F32)],
        2 * lon_all * lon_all * wide,
        2 * lon_all * lon_all + 4 * lon_all * wide,
        14,
    )(place, *moved, *lon, x_packed)


def weigh(place, grads, x_ref, weighted):
    part = place[1]
    depth, lanes = grads[0].shape
    wide = x_ref.shape[1]
    mark = jnp.where(low_lanes((depth, lanes)), 0, 1)
    for t in range(4):
        packed = grads[t % 2][...].astype(F32)
        both = jnp.where(mark == ((part // 2) ^ (t // 2)), packed, swap(packed))
        rows = pl.ds(pl.multiple_of((part ^ t) * depth, depth), depth)
        for b in range(0, wide, lanes):
            weighted[t * depth : (t + 1) * depth, b : b + lanes] = (
                x_ref[rows, b : b + lanes].astype(F32) * both
            ).astype(BF16)


def spread_kernel(group, first, place, *refs):
    if first:
        grads, x_ref, refs = refs[:2], refs[2], refs[3:]
        lon_refs, out_refs, weighted = refs[:4], refs[4:-1], refs[-1]
        weigh(place, grads, x_ref, weighted)
    else:
        weighted, lon_refs, out_refs = refs[0], refs[1:5], refs[5:]
    me, part = place[0], place[1]
    lon_dev = out_refs[0].shape[0]
    depth = lon_refs[0].shape[0]
    for j, s in enumerate(group):
        d = me ^ s
        columns = pl.ds(pl.multiple_of(d * lon_dev, lon_dev), lon_dev)
        start = ((d // 2) ^ part) * depth + (d % 2) * lon_dev
        total = weighted[pl.ds(pl.multiple_of(start, lon_dev), lon_dev), :].astype(F32)
        for t in range(4):
            total = total + lax.dot_general(
                lon_refs[t][:, columns],
                weighted[t * depth : (t + 1) * depth, :],
                (((0,), (0,)), ((), ())),
                preferred_element_type=F32,
            )
        out_refs[j][...] = total.astype(BF16)


def spread_back(group, first, place, inputs, lon, lon_dev):
    lon_all, wide = inputs[-1].shape
    count = len(group)
    block = jax.ShapeDtypeStruct((lon_dev, wide), BF16)
    outs = [block] * count + ([jax.ShapeDtypeStruct((lon_all, wide), BF16)] if first else [])
    return local_call(
        functools.partial(spread_kernel, group, first),
        outs,
        [],
        2 * lon_all * lon_dev * wide * count,
        2 * lon_all * lon_all + 4 * lon_all * wide,
        12,
    )(place, *inputs, *lon)


def contract_kernel(half, sources, columns, pieces, members, last, place, base_ref, *refs):
    count = len(sources)
    messages, refs = refs[:count], refs[count:]
    parts, refs = {half: refs[:pieces]}, refs[pieces:]
    me = place[0]
    lanes = 128
    if last:
        out_hbm, all_ref, lat_ref, left_ref, stage_ref, out_sem = refs
    else:
        out_ref, all_ref, lat_ref, left_ref = refs
    latitude_rows(place, parts, all_ref, [(s, half) for s in sources], lat_ref, columns)
    rows = left_ref.shape[0] // members
    steps = base_ref.shape[1] // rows

    def copy_out(at, slot, i):
        start = pl.multiple_of(at * members * rows, members * rows)
        to_lanes = pl.ds(pl.multiple_of((me ^ columns[i]) * lanes, lanes), lanes)
        return pltpu.make_async_copy(
            stage_ref.at[slot, i],
            out_hbm.at[pl.ds(start, members * rows), to_lanes],
            out_sem.at[slot, i],
        )

    def body(step, carry):
        slot = step % 2
        here = pl.ds(pl.multiple_of(step * rows, rows), rows)
        if last:

            @pl.when(step >= 2)
            def _():
                for i in range(len(columns)):
                    copy_out(step - 2, slot, i).wait()

        def read(j, pair):
            return messages[j][here, pair * lanes : (pair + 1) * lanes].astype(F32)

        for member in range(members):
            for j in range(0, count, 2):
                both = pack(read(j, member // 2), read(j + 1, member // 2), member % 2)
                left_ref[
                    member * rows : (member + 1) * rows, j // 2 * lanes : (j // 2 + 1) * lanes
                ] = both.astype(BF16)
        wide = 256
        for c in range(0, len(columns) * lanes, wide):
            product = jnp.dot(left_ref[...], lat_ref[:, c : c + wide], preferred_element_type=F32)
            for b in range(0, wide, lanes):
                i = (c + b) // lanes
                where = pl.ds(pl.multiple_of((me ^ columns[i]) * lanes, lanes), lanes)
                for k in range(members):
                    value = product[k * rows : (k + 1) * rows, b : b + lanes]
                    if columns[i] in sources:
                        packed = read(sources.index(columns[i]), k // 2)
                        if half != k % 2:
                            packed = swap(packed)
                        mask = low_lanes(packed.shape)
                        zero = jnp.zeros_like(packed)
                        value = value + (
                            jnp.where(mask, zero, packed) if half else jnp.where(mask, packed, zero)
                        )
                    value = value + base_ref[k, here, where].astype(F32)
                    if last:
                        stage_ref[slot, i, pl.ds(k, rows, stride=members), :] = value
                    else:
                        out_ref[k, here, where] = value
                if last:
                    copy_out(step, slot, i).start()
        return carry

    lax.fori_loop(0, steps, body, 0)
    if last:
        for at in (steps - 2, steps - 1):
            for i in range(len(columns)):
                copy_out(at, at % 2, i).wait()


def contract(half, sources, place, base, messages, lat, last):
    members, lon_dev, lat_all = base.shape
    columns = FAR + NEAR
    count = len(sources)
    piece = 128
    rows = 64
    scratch = [
        pltpu.VMEM((4 * piece, lat_all), BF16),
        pltpu.VMEM((count * piece // 2, lat_all), BF16),
        pltpu.VMEM((members * rows, count * piece // 2), BF16),
    ]
    if last:
        out_shape, out_spec = jax.ShapeDtypeStruct((lon_dev * members, lat_all), F32), ANY
        scratch += [
            pltpu.VMEM((2, len(columns), members * rows, piece), F32),
            pltpu.SemaphoreType.DMA((2, len(columns))),
        ]
    else:
        out_shape, out_spec = jax.ShapeDtypeStruct(base.shape, F32), VMEM
    return local_call(
        functools.partial(contract_kernel, half, sources, columns, len(lat[half]), members, last),
        out_shape,
        scratch,
        members * lon_dev * lat_all * count * piece,
        8 * base.size,
        16,
        out_spec,
    )(place, base, *[messages[s] for s in sources], *lat[half])


def exchange(value, axis, size, shift):
    return lax.ppermute(value, axis, [(i, i ^ shift) for i in range(size)])


def local_fast(*args):
    return local_fast_body(*args)


def local_fast_body(controls, perturbations, lat_factor, lon_factor, obs_index, obs_weight, obs_count):
    lon_dev, members, lat_all = controls.shape
    lon_all, _, band = perturbations.shape
    narrow = band // 2
    part, me = lax.axis_index("mem"), lax.axis_index("lon")
    place = jnp.stack([me, part]).astype(jnp.int32)
    split = lat_factor.reshape(lat_factor.shape[0] // band, 2, narrow, lat_all)
    even = me % 2 == 0

    def gathered(value):
        across = exchange(value, "mem", 4, 2)
        beside = exchange(value, "mem", 4, 1)
        return [value, beside, across, exchange(across, "mem", 4, 1)]

    same = [jnp.where(even, split[0, h], split[1, h]) for h in range(2)]
    other = [jnp.where(even, split[1, h], split[0, h]) for h in range(2)]
    lat_a, lat_b = gathered(same[0]), gathered(other[0])
    lat = [lat_a + lat_b, gathered(jnp.concatenate([same[1], other[1]], axis=0))]
    lon = gathered(lon_factor)
    x_packed = prepare_perturbations(perturbations)
    own_map = weight_map(obs_index, obs_weight, obs_count, lon_all // 4, band)
    other_map = exchange(own_map, "mem", 4, 2)
    first_side = part < 2
    low_map = jnp.where(first_side, own_map, other_map)
    high_map = jnp.where(first_side, other_map, own_map)

    def sent(group, blocks):
        return {s: exchange(block, "lon", 8, s) if s else block for s, block in zip(group, blocks)}

    far = [{}, {}]
    for group, parts in ((FIRST, lat_a), (SECOND, lat_b)):
        far[0] |= sent(group, banded((0,), group, place, controls, {0: parts}))
    far[1] = sent(FAR, banded((1,), FAR, place, controls, {1: lat[1]}))
    for h in range(2):
        blocks = banded((h,), NEAR, place, controls, {h: lat[h]})
        far[h] |= sent(NEAR, blocks)
    base = prepare_controls(controls)
    for h in range(2):
        moved = [far[h][s] for s in range(8)]
        send, keep = increment(h, place, moved, lon, x_packed[h])
        keep = keep + exchange(send, "mem", 4, 1)
        keep = keep + exchange(keep, "mem", 4, 2)
        cells = slice(h * narrow, (h + 1) * narrow)
        weights = jnp.concatenate([low_map[:, cells], high_map[:, cells]], axis=1)
        own = (keep * weights).astype(BF16)
        other = exchange(own, "mem", 4, 1)
        *blocks, weighted = spread_back(FAR, True, place, [own, other, x_packed[h]], lon, lon_dev)
        back = sent(FAR, blocks)
        blocks = spread_back(NEAR, False, place, [weighted], lon, lon_dev)
        back |= sent(NEAR, blocks)
        for name, sources in (("sum0", FAR + NEAR),) if h == 0 else (("sum1", NEAR), ("sum2", FAR)):
            base = contract(h, sources, place, base, back, lat, name == "sum2")
    return base.reshape(lon_dev, members, lat_all)


def local_plain(controls, perturbations, lat_factor, lon_factor, obs_index, obs_weight, obs_count):
    lon_dev, mem_dev, lat_all = controls.shape
    lat_full = lax.all_gather(lat_factor, "mem", axis=0, tiled=True)
    control_rows = controls.reshape(lon_dev * mem_dev, lat_all)
    band_rows = (
        control_rows.astype(F32)
        + lax.dot_general(
            control_rows, lat_full, (((1,), (1,)), ((), ())), preferred_element_type=F32
        )
    ).astype(BF16)
    moved = lax.all_to_all(
        band_rows.reshape(lon_dev, mem_dev, lat_all), "lon", split_axis=2, concat_axis=0, tiled=True
    )
    lon_all, _, lat_band = moved.shape
    columns = moved.reshape(lon_all, mem_dev * lat_band)
    lon_full = lax.all_gather(lon_factor, "mem", axis=0, tiled=True)
    localized = columns.astype(F32) + jnp.dot(lon_full, columns, preferred_element_type=F32)
    weighted_fwd = perturbations.reshape(lon_all, mem_dev * lat_band).astype(F32) * localized
    partial_sum = jnp.sum(weighted_fwd.reshape(lon_all, mem_dev, lat_band), axis=1)
    tile_sum = lax.psum_scatter(partial_sum, "mem", scatter_dimension=0, tiled=True)
    weights = weight_map(obs_index, obs_weight, obs_count, tile_sum.shape[0], lat_band)
    grad_tile = (tile_sum * weights).astype(BF16)
    gradient = lax.all_gather(grad_tile, "mem", axis=0, tiled=True)
    weighted = (
        (perturbations.astype(F32) * gradient.astype(F32)[:, None, :])
        .astype(BF16)
        .reshape(lon_all, mem_dev * lat_band)
    )
    back = lax.dot_general(
        lon_full, weighted, (((0,), (0,)), ((), ())), preferred_element_type=F32
    )
    spread = (weighted.astype(F32) + back).astype(BF16).reshape(lon_all, mem_dev, lat_band)
    returned = lax.all_to_all(spread, "lon", split_axis=0, concat_axis=2, tiled=True)
    back_rows = returned.reshape(lon_dev * mem_dev, lat_all)
    result = (
        control_rows.astype(F32)
        + back_rows.astype(F32)
        + jnp.dot(back_rows, lat_full, preferred_element_type=F32)
    )
    return result.reshape(lon_dev, mem_dev, lat_all)


def solution(mesh):
    in_specs = (
        P("lon", "mem", None),
        P(None, "mem", "lon"),
        P("mem", None),
        P("mem", None),
        P("mem", "lon", None),
        P("mem", "lon", None),
        P("mem", "lon"),
    )
    out_specs = P("lon", "mem", None)
    few = mesh.shape["mem"] == 4 and mesh.shape["lon"] == 8

    def local(controls, perturbations, lat_factor, *rest):
        lon_dev, members, _ = controls.shape
        lon_all, _, band = perturbations.shape
        fits = (
            few
            and band == 128
            and members == 8
            and lat_factor.shape[0] == 2 * band
            and lon_dev == 256
            and lon_all == 8 * lon_dev
        )
        plan = local_fast if fits else local_plain
        return plan(controls, perturbations, lat_factor, *rest)

    return jax.shard_map(local, mesh=mesh, in_specs=in_specs, out_specs=out_specs, check_vma=False)
```
